256 devices in a mesh: pp: 2 (over y_hi), cp: 32 (over x, z), tp: 4 (over y_lo, core).
Axes of the slice: x: 4, y: 4 (y_hi: 2, y_lo: 2; y = y_hi * 2 + y_lo), z: 8, core: 2. Of those that a mesh axis runs over, the one named last changes fastest.
Arguments:
- queries: bfloat16 [2, 4096, 8192], P('pp', 'cp', 'tp'), may hold values from -9 to 9
- key_vectors: bfloat16 [2, 4096, 512], P('pp', 'cp', 'tp'), may hold values from -6 to 6
- value_vectors: bfloat16 [2, 4096, 512], P('pp', 'cp', 'tp'), may hold values from -30 to 30
- block_order: int32 [64], replicated, may hold values from 0 to 63, each once
- norm_gain: bfloat16 [2, 8192], P('pp', 'tp'), may hold values from 0.099609375 to 1.8984375
- kv_weight: bfloat16 [2, 8192, 1024], P('pp', 'tp'), may hold values from -0.0625 to 0.0625
Outputs:
- max_logits: float32 [2, 64], P('pp', 'tp')
- kv_next: bfloat16 [2, 4096, 1024], P('pp', 'cp', 'tp')
The draws below stay inside these ranges and needn't reach their ends.
Inputs may be any that keep to these rules, and one draw needn't show every extreme that they name: A permutation; rows 2 c * 64 to (2 c + 2) * 64 - 1 hold the positions of blocks block_order[2 c] and block_order[2 c + 1], in that order.
All inputs are finite; a program needn't handle non-finite values.
Results may differ from the reference program's by a relative error of at most 0.018.
Values may be sent and summed in bfloat16 or wider, within the bound.
A program may use at most 128 MiB of HBM per device.

```python
import math
import jax
import jax.numpy as jnp
from jax import lax

H = 64
KVH = 4
DH = 128
SECTIONS = 2
TOKENS = 4096
BLOCK = 64
N_CP = 32


def draw_queries(key, part):
    base = jnp.clip(jax.random.normal(jax.random.fold_in(key, 1), (SECTIONS, TOKENS, H * DH), jnp.float32), -6.0, 6.0)
    return base.astype(jnp.bfloat16)


def draw_key_vectors(key, part):
    base = jnp.clip(jax.random.normal(jax.random.fold_in(key, 2), (SECTIONS, TOKENS, KVH * DH), jnp.float32), -6.0, 6.0)
    return base.astype(jnp.bfloat16)


def draw_value_vectors(key, part):
    head_ids = (jnp.arange(KVH * DH) // DH).astype(jnp.float32)
    steps_total = max(KVH - 1, 1)
    base = jnp.clip(jax.random.normal(jax.random.fold_in(key, 5), (SECTIONS, TOKENS, KVH * DH), jnp.float32), -4.0, 4.0)
    return (base * 3.0 ** (head_ids / steps_total)).astype(jnp.bfloat16)


def steps_of(own_key, extent, cuts, least, largest):
    def one(dim, blocks):
        heights = jax.random.uniform(jax.random.fold_in(jax.random.fold_in(own_key, 6), dim), (blocks,), jnp.float32, least / len(cuts), largest / len(cuts))
        return jnp.repeat(jnp.exp(heights), extent[dim] // blocks).reshape((-1,) + (1,) * (len(extent) - dim - 1))

    factor_of = one(*cuts[0])
    for cut in cuts[1:]:
        factor_of = factor_of * one(*cut)
    return factor_of


def noise(stream_key, extent, scale, bound, cuts=(), kind=jnp.bfloat16):
    loudness = steps_of(stream_key, extent, cuts, -0.22, 0.18) if cuts else 1.0
    array = jax.random.normal(stream_key, extent, jnp.float32) * scale * loudness
    return jnp.minimum(jnp.maximum(array, -bound), bound).astype(kind)


def setup_inputs(seed: int = 0) -> dict:
    key_list = jax.random.split(jax.random.key(seed), 7)
    return {
        "queries": draw_queries(jax.random.fold_in(key_list[6], 71), 0),
        "key_vectors": draw_key_vectors(jax.random.fold_in(key_list[6], 71), 0),
        "value_vectors": draw_value_vectors(jax.random.fold_in(key_list[6], 71), 0),
        "block_order": jax.random.permutation(key_list[3], 2 * N_CP).astype(jnp.int32),
        "norm_gain": jnp.clip(1.0 + 0.18 * jax.random.normal(key_list[4], (SECTIONS, H * DH), jnp.float32), 0.099609375, 1.8984375).astype(jnp.bfloat16),
        "kv_weight": noise(key_list[5], (SECTIONS, H * DH, 2 * KVH * DH), (H * DH) ** -0.5, 0.0625, ((0, 2), (1, 4))),
    }


def reference(queries, key_vectors, value_vectors, block_order, norm_gain, kv_weight):
    row_ids = jnp.arange(TOKENS, dtype=jnp.int32)
    positions = block_order[row_ids // BLOCK].astype(jnp.int32) * BLOCK + row_ids % BLOCK
    allowed = positions[None, :] <= positions[:, None]
    group_size = H // KVH
    score_scale = 1.0 / math.sqrt(DH)
    highest = lax.Precision.HIGHEST
    contexts = []
    peaks = []
    for section in range(SECTIONS):
        q_all = queries[section].reshape(TOKENS, H, DH).astype(jnp.float32)
        k_all = key_vectors[section].reshape(TOKENS, KVH, DH).astype(jnp.float32)
        v_all = value_vectors[section].reshape(TOKENS, KVH, DH).astype(jnp.float32)

        def one_head(head_index):
            q_head = lax.dynamic_index_in_dim(q_all, head_index, 1, keepdims=False)
            k_head = lax.dynamic_index_in_dim(k_all, head_index // group_size, 1, keepdims=False)
            v_head = lax.dynamic_index_in_dim(v_all, head_index // group_size, 1, keepdims=False)
            scores = jnp.dot(q_head, k_head.T, precision=highest) * score_scale
            masked = jnp.where(allowed, scores, -jnp.inf)
            rowmax = lax.optimization_barrier(jnp.max(masked, axis=1))
            exponent = jnp.where(allowed, jnp.exp(masked - rowmax[:, None]), 0.0)
            probs = exponent.astype(jnp.bfloat16).astype(jnp.float32)
            context = jnp.dot(probs, v_head, precision=highest) / lax.optimization_barrier(jnp.sum(exponent, axis=1))[:, None]
            return (context, jnp.max(rowmax))
        context, peak = lax.map(one_head, jnp.arange(H, dtype=jnp.int32))
        attn = jnp.transpose(context, (1, 0, 2)).reshape(TOKENS, H * DH).astype(jnp.bfloat16)
        contexts.append(attn)
        peaks.append(peak)
    max_logits = jnp.stack(peaks)
    results = []
    for section in range(SECTIONS):
        handed = contexts[(section - 1) % SECTIONS]
        wide = handed.astype(jnp.float32)
        mean_square = lax.optimization_barrier(jnp.mean(wide * wide, axis=1, keepdims=True))
        normed = (wide * lax.rsqrt(mean_square + 1e-05) * norm_gain[section].astype(jnp.float32)[None, :]).astype(jnp.bfloat16)
        results.append(jnp.dot(normed, kv_weight[section], preferred_element_type=jnp.float32).astype(jnp.bfloat16))
    kv_next = jnp.stack(results)
    return (max_logits, kv_next)
```

```python
import math

import jax
import jax.numpy as jnp
from jax import lax
from jax.experimental import pallas as pl
from jax.experimental.pallas import tpu as pltpu
from jax.sharding import PartitionSpec as P

BF = jnp.bfloat16
F32 = jnp.float32
MESH = pl.DeviceIdType.MESH

DH = 128
ROWS = 128
HALF = 64
HEADS = 16
NX, NZ = 4, 8
SLOTS = NX * NZ
FEATURES = 8192
GROUP = 4
TQ = GROUP * ROWS
TK = 1024
VROWS = 144
COLS = 1024
OUT = 256
BIG = 2.0**100
SCALE = 1.0 / math.sqrt(DH)
EXP2 = SCALE * math.log2(math.e)
N_SEM = 128


def device(y, x, z, c):
    return ((y % 4) // 2, (x % NX) * NZ + z % NZ, (y % 2) * 2 + c)


class Traffic:
    def __init__(self, send, recv):
        self.send, self.recv = send, recv
        self.copies = {}
        self.after = {}
        self.need = {}
        self.order = []

    def add(self, name, src, dst, to, after=()):
        i = len(self.copies)
        self.copies[name] = pltpu.make_async_remote_copy(
            src_ref=src,
            dst_ref=dst,
            send_sem=self.send.at[i],
            recv_sem=self.recv.at[i],
            device_id=to,
            device_id_type=MESH,
        )
        self.need[name] = set(after)
        for a in after:
            self.after.setdefault(a, []).append(name)

    def start(self, name):
        self.copies[name].start()

    def arrive(self, name):
        self.copies[name].wait_recv()
        for child in self.after.get(name, ()):
            self.need[child].discard(name)
            if not self.need[child]:
                self.start(child)

    def sent(self):
        for c in self.copies.values():
            c.wait_send()


def kernel(
    order, q_hbm, k_hbm, v_ref, gain_ref, w_hbm,
    kv_out, max_out,
    kbuf, vt, vown, qs, w, s_buf, acc_out, parts, got, sqbuf, sqgot, mxbuf, mxgot, mx2, mxgot2,
    send, recv, local,
):
    pp, cp, tp = lax.axis_index("pp"), lax.axis_index("cp"), lax.axis_index("tp")
    y, x, z, c = pp * 2 + tp // 2, cp // NZ, cp % NZ, tp % 2

    wcopy = pltpu.make_async_copy(w_hbm, w, local.at[0])
    wcopy.start()

    barrier = pltpu.get_barrier_semaphore()
    peers = [device(y, x + d, z, c) for d in (1, 2, 3)]
    peers += [device(y, x, z + d, c) for d in (1, 2, 6, 7)]
    peers += [device(y + 2, x, z + d, c) for d in range(NZ)]
    mates = [device(y, x, z, 1 - c), device(y // 2 * 2 + 1 - y % 2, x, z, c)]
    mates += [device(y // 2 * 2 + 1 - y % 2, x, z, 1 - c)]
    for d in peers + mates:
        pl.semaphore_signal(barrier, inc=1, device_id=d, device_id_type=MESH)

    vown[...] = v_ref[...].astype(F32).T.astype(BF)

    t = Traffic(send, recv)

    def ks(dz, dx, lo=0, n=ROWS):
        return kbuf.at[pl.ds(((dz % NZ) * NX + dx % NX) * ROWS + lo, n), pl.ds(0, DH)]

    def vs(dz, dx, lo=0, n=DH):
        return vt.at[(dz % NZ) * NX + dx % NX, pl.ds(lo, n), :]

    partner = device(y + 2, x, z, c)
    t.add("k", k_hbm, ks(0, 0), partner)
    t.add("v", vown, vs(0, 0), partner)
    for h in range(HEADS):
        t.add(
            ("q", h),
            q_hbm.at[:, pl.ds(h * DH, DH)],
            qs.at[pl.ds(h * ROWS, ROWS), pl.ds(0, DH)],
            partner,
        )
    for d in (1, 3, 2):
        t.add(("kx", d), ks(0, 0), ks(0, -d), device(y, x + d, z, c), ["k"])
    for s in range(4):
        for dx in (0, 1, 3, 2):
            first = ["k"] if dx == 0 else [("kx", 4 - dx)]
            n, lo = (ROWS, 0) if s < 3 else (HALF, HALF)
            t.add(
                ("ku", s, dx), ks(-s, dx, 0, n), ks(-s - 1, dx, 0, n),
                device(y, x, z + 1, c), first if s == 0 else [("ku", s - 1, dx)],
            )
            t.add(
                ("kd", s, dx), ks(s, dx, lo, n), ks(s + 1, dx, lo, n),
                device(y, x, z - 1, c), first if s == 0 else [("kd", s - 1, dx)],
            )
    for d in (1, -1, 2, -2):
        t.add(("vz", d), vs(0, 0), vs(-d, 0), device(y, x, z + d, c), ["v"])
    for d in (1, -1):
        lo = 0 if d > 0 else HALF
        t.add(("vz", 3 * d), vs(-2 * d, 0), vs(-3 * d, 0), device(y, x, z + d, c), [("vz", 2 * d)])
        t.add(
            ("vz", 4 * d), vs(-2 * d, 0, lo, HALF), vs(-4 * d, 0, lo, HALF),
            device(y, x, z + 2 * d, c), [("vz", 2 * d)],
        )
    for dz in (0, 1, -1, 2, -2, 3, -3, 4):
        came = ["v"] if dz == 0 else [("vz", 4), ("vz", -4)] if dz == 4 else [("vz", -dz)]
        for d in (1, 3, 2):
            t.add(("vx", dz, d), vs(dz, 0), vs(dz, -d), device(y, x + d, z, c), came)

    pl.semaphore_wait(barrier, len(peers) + len(mates))

    for name in ["k", "v"] + [("q", h) for h in range(HEADS)]:
        t.start(name)

    row = lax.broadcasted_iota(jnp.int32, (ROWS, DH), 0)
    lane = lax.broadcasted_iota(jnp.int32, (ROWS, DH), 1)
    mine = (lane >= HALF) == (row >= HALF)
    off = lane % HALF
    q_mask = jnp.where(mine & ((off == 0) | (off > row % HALF)), -BIG, 0.0).astype(BF)
    for h in range(HEADS):
        qs[pl.ds(h * ROWS, ROWS), pl.ds(DH, DH)] = q_mask
    hrow = lax.broadcasted_iota(jnp.int32, (HALF, DH), 0)
    hlane = lax.broadcasted_iota(jnp.int32, (HALF, DH), 1)
    hoff = hlane % HALF
    after_all = (hoff == 0).astype(F32)
    in_block = ((hoff == hrow) & (hoff > 0)).astype(F32)
    half_id = jnp.where(hlane < HALF, order[2 * cp], order[2 * cp + 1])
    for slot in range(SLOTS):
        dz, dx = slot // NX, slot % NX
        src = ((x + dx) % NX) * NZ + (z + dz) % NZ
        for b in range(2):
            block = order[2 * src + b]
            k_mask = jnp.where(half_id < block, after_all, jnp.where(half_id == block, in_block, 0.0))
            kbuf[pl.ds(slot * ROWS + b * HALF, HALF), pl.ds(DH, DH)] = k_mask.astype(BF)
        vt[slot, pl.ds(DH, VROWS - DH), :] = jnp.ones((VROWS - DH, ROWS), BF)

    t.arrive("k")
    t.arrive("v")
    for d in (1, 3, 2):
        t.arrive(("kx", d))
    for d in (1, -1, 2, -2):
        t.arrive(("vz", d))
    for s in range(4):
        for dx in (0, 1, 3, 2):
            t.arrive(("ku", s, dx))
            t.arrive(("kd", s, dx))
        if s == 0:
            for d in (3, -3, 4, -4):
                t.arrive(("vz", d))
    for dz in (0, 1, -1, 2, -2, 3, -3, 4):
        for d in (1, 3, 2):
            t.arrive(("vx", dz, d))
    for h in range(HEADS):
        t.arrive(("q", h))
    wcopy.wait()

    steps = SLOTS * ROWS // TK
    per = TK // ROWS

    def score(first, j, slot):
        s = lax.dot_general(
            kbuf[pl.ds(j * TK, TK), :], qs[pl.ds(first, TQ), :],
            (((1,), (1,)), ((), ())), preferred_element_type=F32,
        )
        s_buf[slot] = s
        return jnp.max(s, axis=0, keepdims=True)

    acc_out[...] = jnp.zeros_like(acc_out)
    sqbuf[...] = jnp.zeros_like(sqbuf)
    mxbuf[...] = jnp.full_like(mxbuf, -BIG)
    groups = HEADS // GROUP
    mlane = lax.broadcasted_iota(jnp.int32, (8, DH), 1)

    def group(g, peak):
        first = pl.multiple_of(g * TQ, TQ)
        following = pl.multiple_of(jnp.minimum(g + 1, groups - 1) * TQ, TQ)
        top = total = None
        for j in range(steps):
            new_top = peak if j == 0 else jnp.maximum(top, peak)
            p = jnp.exp2((s_buf[j % 2] - new_top) * EXP2).astype(BF)
            if j < steps - 1:
                peak = score(first, j + 1, (j + 1) % 2)
            else:
                peak = score(following, 0, (j + 1) % 2)
            values = jnp.concatenate([vt[j * per + i] for i in range(per)], axis=1)
            part = jnp.dot(values, p, preferred_element_type=F32)
            total = part if j == 0 else total * jnp.exp2((top - new_top) * EXP2) + part
            top = new_top
        attn = (total[:DH, :] / total[DH : DH + 1, :]).astype(BF).astype(F32)
        square = jnp.sum(attn * attn, axis=0, keepdims=True)
        pieces = []
        for i in range(GROUP):
            cut = slice(i * ROWS, (i + 1) * ROWS)
            sqbuf[...] += jnp.broadcast_to(square[:, cut], (8, ROWS))
            best = jnp.max(top[:, cut], axis=1, keepdims=True) * SCALE
            mxbuf[...] = jnp.where(mlane == g * GROUP + i, best, mxbuf[...])
            gain = gain_ref[pl.ds(g * GROUP + i, 1), :]
            pieces.append((attn[:, cut].T * gain).astype(BF))
        acc_out[...] += jnp.dot(
            jnp.concatenate(pieces, axis=1), w[pl.ds(first, TQ), :], preferred_element_type=F32
        )
        return peak

    lax.fori_loop(0, groups, group, score(0, 0, 0))

    for d in (1, 2, 3):
        t.add(("mx", d), mxbuf, mxgot.at[d], device(y, x + d, z, c))
        t.start(("mx", d))
    for j in range(4):
        parts[j] = acc_out[:, pl.ds(j * OUT, OUT)].astype(BF)
    for i, to in reversed(list(enumerate(mates))):
        t.add(("sq", i), sqbuf, sqgot.at[i], to)
        t.add(("rs", i), parts.at[to[2]], got.at[i], to)
        t.start(("sq", i))
        t.start(("rs", i))
    for d in (1, 2, 3):
        t.arrive(("mx", d))
    mx2[...] = jnp.maximum(jnp.maximum(mxbuf[...], mxgot[1]), jnp.maximum(mxgot[2], mxgot[3]))
    for d in range(NZ):
        t.add(("mz", d), mx2, mxgot2.at[d], device(y + 2, x, z + d, c))
        t.start(("mz", d))
    for i in range(3):
        t.arrive(("sq", i))
        t.arrive(("rs", i))
    square = sqbuf[...] + sqgot[0] + sqgot[1] + sqgot[2]
    inverse = lax.rsqrt(square * (1.0 / FEATURES) + 1e-05)
    inverse = jnp.broadcast_to(inverse[:1, :], (ROWS, ROWS)).T
    own = parts[tp].astype(F32)
    result = own + got[0].astype(F32) + got[1].astype(F32) + got[2].astype(F32)
    kv_out[...] = (result * jnp.concatenate([inverse, inverse], axis=1)).astype(BF)
    for d in range(NZ):
        t.arrive(("mz", d))
    best = mxgot2[0]
    for d in range(1, NZ):
        best = jnp.maximum(best, mxgot2[d])
    max_out[...] = best
    t.sent()


def on_device(queries, key_vectors, value_vectors, block_order, norm_gain, kv_weight):
    any_ = pl.BlockSpec(memory_space=pl.ANY)
    vmem = pl.BlockSpec(memory_space=pltpu.VMEM)
    kv, peak = pl.pallas_call(
        kernel,
        out_shape=(jax.ShapeDtypeStruct((ROWS, OUT), BF), jax.ShapeDtypeStruct((8, DH), F32)),
        in_specs=[pl.BlockSpec(memory_space=pltpu.SMEM), any_, any_, vmem, vmem, any_],
        out_specs=(vmem, vmem),
        scratch_shapes=[
            pltpu.VMEM((SLOTS * ROWS, 2 * DH), BF),
            pltpu.VMEM((SLOTS, VROWS, ROWS), BF),
            pltpu.VMEM((DH, ROWS), BF),
            pltpu.VMEM((HEADS * ROWS, 2 * DH), BF),
            pltpu.VMEM((HEADS * DH, COLS), BF),
            pltpu.VMEM((2, TK, TQ), F32),
            pltpu.VMEM((ROWS, COLS), F32),
            pltpu.VMEM((4, ROWS, OUT), BF),
            pltpu.VMEM((3, ROWS, OUT), BF),
            pltpu.VMEM((8, DH), F32),
            pltpu.VMEM((3, 8, DH), F32),
            pltpu.VMEM((8, DH), F32),
            pltpu.VMEM((4, 8, DH), F32),
            pltpu.VMEM((8, DH), F32),
            pltpu.VMEM((NZ, 8, DH), F32),
            pltpu.SemaphoreType.DMA((N_SEM,)),
            pltpu.SemaphoreType.DMA((N_SEM,)),
            pltpu.SemaphoreType.DMA((1,)),
        ],
        compiler_params=pltpu.CompilerParams(
            collective_id=0, has_side_effects=True, vmem_limit_bytes=48 << 20
        ),
        name="attention",
    )(
        block_order,
        queries[0],
        key_vectors[0],
        value_vectors[0],
        norm_gain[0].astype(F32).reshape(HEADS, DH),
        kv_weight[0],
    )
    return peak[:1, :HEADS], kv[None]


def solution(mesh):
    return jax.shard_map(
        on_device,
        mesh=mesh,
        in_specs=(
            P("pp", "cp", "tp"),
            P("pp", "cp", "tp"),
            P("pp", "cp", "tp"),
            P(),
            P("pp", "tp"),
            P("pp", "tp", None),
        ),
        out_specs=(P("pp", "tp"), P("pp", "cp", "tp")),
        check_vma=False,
    )
```

```python
import math

import jax
import jax.numpy as jnp
from jax import lax
from jax.experimental import pallas as pl
from jax.experimental.pallas import tpu as pltpu
from jax.sharding import PartitionSpec as P

BF = jnp.bfloat16
F32 = jnp.float32
MESH = pl.DeviceIdType.MESH

DH = 128
ROWS = 128
HALF = 64
HEADS = 16
NX, NZ = 4, 8
SLOTS = NX * NZ
FEATURES = 8192
GROUP = 4
TQ = GROUP * ROWS
TK = 6 * ROWS
VROWS = 144
COLS = 1024
OUT = 256
BIG = 2.0**100
SCALE = 1.0 / math.sqrt(DH)
EXP2 = SCALE * math.log2(math.e)
N_SEM = 128
VMEM_LIMIT = 57 << 20
TILES = (
    [(0, dx) for dx in range(NX)],
    [(1, 0), (-1, 0), (2, 0), (-2, 0)],
    [(dz, dx) for dx in (1, 3, 2) for dz in (1, -1)],
    [(dz, dx) for dx in (1, 3, 2) for dz in (2, -2)],
    [(dz, dx) for dx in (0, 1, 3, 2) for dz in (3, -3)],
    [(4, dx) for dx in range(NX)],
)
SLOT = {(dz % NZ, dx): i for i, (dz, dx) in enumerate(sum(TILES, []))}
FIRST = [SLOT[t[0][0] % NZ, t[0][1]] for t in TILES]
SIZE = [len(t) for t in TILES]
LATE = 4


def ring(i, *dxs):
    return ("arrive", *[(a, i, dx) for dx in dxs for a in ("ku", "kd")])


SCHEDULE = (
    [("arrive", ("kx", 3), ("kx", 1), ("kx", 2))]
    + [("arrive", ("vz", 2), ("vz", -2), ("vz", 1), ("vz", -1)), ring(0, 0)]
    + [(0, 0), ("flush",), ("arrive", ("vz", 3), ("vz", -3), ("vz", 4), ("vz", -4))]
    + [ring(0, 1, 3, 2), ring(1, 0)]
    + [(1, 0), (0, 1), (1, 1), (2, 0), (2, 1), (0, 2), ring(1, 1, 3), (1, 2), ring(1, 2)]
    + [(2, 2), ring(2, 0), (3, 0), (3, 1), (3, 2), (0, 3), ring(2, 1, 3), (1, 3), ring(2, 2)]
    + [(2, 3), (3, 3)]
)


def slot_of(dz, dx):
    return SLOT[dz % NZ, dx % NX]


def device(y, x, z, c):
    return ((y % 4) // 2, (x % NX) * NZ + z % NZ, (y % 2) * 2 + c)


class Traffic:
    def __init__(self, send, recv):
        self.send, self.recv = send, recv
        self.copies = {}
        self.after = {}
        self.need = {}
        self.came = set()
        self.started = []

    def add(self, name, src, dst, to, after=()):
        i = len(self.copies)
        self.copies[name] = pltpu.make_async_remote_copy(
            src_ref=src,
            dst_ref=dst,
            send_sem=self.send.at[i],
            recv_sem=self.recv.at[i],
            device_id=to,
            device_id_type=MESH,
        )
        self.need[name] = set(after)
        for a in after:
            self.after.setdefault(a, []).append(name)

    def start(self, name):
        self.copies[name].start()
        self.started.append(name)

    def arrive(self, *names):
        for name in names:
            if name in self.came:
                continue
            self.came.add(name)
            self.copies[name].wait_recv()
            for child in self.after.get(name, ()):
                self.need[child].discard(name)
                if not self.need[child]:
                    self.start(child)

    def sent(self):
        for name in self.started:
            self.copies[name].wait_send()
        self.started = []


def kernel(
    order, gain_ref, q_hbm, k_hbm, v_hbm, w_hbm,
    kv_out, max_out,
    kbuf, vt, vin, vown, qs, w, s_buf, s_late, tops, totals, acc_out, parts, got,
    sqbuf, sqgot, mxbuf, mxgot, mx2, mxgot2, send, recv, local,
):
    pp, cp, tp = lax.axis_index("pp"), lax.axis_index("cp"), lax.axis_index("tp")
    y, x, z, c = pp * 2 + tp // 2, cp // NZ, cp % NZ, tp % 2

    vcopy = pltpu.make_async_copy(v_hbm, vin, local.at[1])
    vcopy.start()
    barrier = pltpu.get_barrier_semaphore()
    peers = [device(y, x + d, z, c) for d in (1, 2, 3)]
    peers += [device(y, x, z + d, c) for d in (1, 2, 6, 7)]
    peers += [device(y + 2, x, z + d, c) for d in range(NZ)]
    other = y // 2 * 2 + 1 - y % 2
    mates = [device(y, x, z, 1 - c), device(other, x, z, c), device(other, x, z, 1 - c)]
    for d in peers + mates:
        pl.semaphore_signal(barrier, inc=1, device_id=d, device_id_type=MESH)
    wcopy = pltpu.make_async_copy(w_hbm, w, local.at[0])
    wcopy.start()

    vcopy.wait()
    vown[...] = vin[...].astype(F32).T.astype(BF)

    t = Traffic(send, recv)

    def ks(dz, dx, lo=0, n=ROWS):
        return kbuf.at[pl.ds(slot_of(dz, dx) * ROWS + lo, n), pl.ds(0, DH)]

    def vs(dz, dx, lo=0, n=DH):
        return vt.at[slot_of(dz, dx), pl.ds(lo, n), :]

    partner = device(y + 2, x, z, c)
    t.add("k", k_hbm, ks(0, 0), partner)
    t.add("v", vown, vs(0, 0), partner)
    for h in range(HEADS):
        t.add(
            ("q", h),
            q_hbm.at[:, pl.ds(h * DH, DH)],
            qs.at[pl.ds(h * ROWS, ROWS), pl.ds(0, DH)],
            partner,
        )
    for d in (1, -1, 2, -2):
        t.add(("vz", d), vs(0, 0), vs(-d, 0), device(y, x, z + d, c), ["v"])
    for d in (1, 3, 2):
        t.add(("kx", d), ks(0, 0), ks(0, -d), device(y, x + d, z, c), ["k"])
    for d in (1, -1):
        lo = 0 if d > 0 else HALF
        far, near = device(y, x, z + 2 * d, c), device(y, x, z + d, c)
        t.add(("vz", 3 * d), vs(-2 * d, 0), vs(-3 * d, 0), near, [("vz", 2 * d)])
        t.add(("vz", 4 * d), vs(-2 * d, 0, lo, HALF), vs(4, 0, lo, HALF), far, [("vz", 2 * d)])
    for i in range(4):
        for dx in (0, 1, 3, 2):
            first = ["k"] if dx == 0 else [("kx", 4 - dx)]
            n, lo = (ROWS, 0) if i < 3 else (HALF, HALF)
            t.add(
                ("ku", i, dx), ks(-i, dx, 0, n), ks(-i - 1, dx, 0, n),
                device(y, x, z + 1, c), first if i == 0 else [("ku", i - 1, dx)],
            )
            t.add(
                ("kd", i, dx), ks(i, dx, lo, n), ks(i + 1, dx, lo, n),
                device(y, x, z - 1, c), first if i == 0 else [("kd", i - 1, dx)],
            )
    for dz in (0, 1, -1, 2, -2, 3, -3, 4):
        came = ["v"] if dz == 0 else [("vz", 4), ("vz", -4)] if dz == 4 else [("vz", -dz)]
        for d in (1, 3, 2):
            t.add(("vx", dz, d), vs(dz, 0), vs(dz, -d), device(y, x + d, z, c), came)

    pl.semaphore_wait(barrier, len(peers) + len(mates))

    for name in ["k", "v"] + [("q", h) for h in range(HEADS)]:
        t.start(name)

    row = lax.broadcasted_iota(jnp.int32, (ROWS, DH), 0)
    lane = lax.broadcasted_iota(jnp.int32, (ROWS, DH), 1)
    mine = (lane >= HALF) == (row >= HALF)
    off = lane % HALF
    q_mask = jnp.where(mine & ((off == 0) | (off > row % HALF)), -BIG, 0.0).astype(BF)
    for h in range(HEADS):
        qs[pl.ds(h * ROWS, ROWS), pl.ds(DH, DH)] = q_mask
    hrow = lax.broadcasted_iota(jnp.int32, (HALF, DH), 0)
    hlane = lax.broadcasted_iota(jnp.int32, (HALF, DH), 1)
    hoff = hlane % HALF
    after_all = (hoff == 0).astype(F32)
    in_block = ((hoff == hrow) & (hoff > 0)).astype(F32)
    half_id = jnp.where(hlane < HALF, order[2 * cp], order[2 * cp + 1])

    def masks(dz):
        for dx in range(NX):
            slot = slot_of(dz, dx)
            src = ((x + dx) % NX) * NZ + (z + dz) % NZ
            for b in range(2):
                block = order[2 * src + b]
                k_mask = jnp.where(half_id < block, after_all, jnp.where(half_id == block, in_block, 0.0))
                kbuf[pl.ds(slot * ROWS + b * HALF, HALF), pl.ds(DH, DH)] = k_mask.astype(BF)
            vt[slot, pl.ds(DH, VROWS - DH), :] = jnp.ones((VROWS - DH, ROWS), BF)

    for dz in range(NZ):
        masks(dz)
    acc_out[...] = jnp.zeros_like(acc_out)
    sqbuf[...] = jnp.zeros_like(sqbuf)
    mxbuf[...] = jnp.full_like(mxbuf, -BIG)
    mlane = lax.broadcasted_iota(jnp.int32, (8, DH), 1)
    t.arrive("k", "v")

    def score(g, tile, into):
        first, size = FIRST[tile] * ROWS, SIZE[tile] * ROWS
        s = lax.dot_general(
            kbuf[pl.ds(first, size), :], qs[pl.ds(g * TQ, TQ), :],
            (((1,), (1,)), ((), ())), preferred_element_type=F32,
        )
        into[...] = s
        return jnp.max(s, axis=0, keepdims=True)

    def ready(g, tile):
        t.arrive(*[("q", h) for h in range(g * GROUP, (g + 1) * GROUP)])
        for dz, dx in TILES[tile]:
            if dz == 0:
                t.arrive("k" if dx == 0 else ("kx", 4 - dx))
            elif dz == 4:
                t.arrive(("ku", 3, dx), ("kd", 3, dx))
            else:
                t.arrive(("kd" if dz > 0 else "ku", abs(dz) - 1, dx))

    def ready_v(tile):
        for dz, dx in TILES[tile]:
            t.arrive(*(["v"] if dz == 0 else [("vz", 4), ("vz", -4)] if dz == 4 else [("vz", -dz)]))
            if dx:
                t.arrive(("vx", dz, 4 - dx))

    def weigh(g, first, size, scores, top, ahead=()):
        p = jnp.exp2((scores[...] - top) * EXP2).astype(BF)
        peaks = [score(*a) for a in ahead]
        values = jnp.concatenate([vt[first + i] for i in range(size)], axis=1)
        part = jnp.dot(values, p, preferred_element_type=F32)
        if g in seen:
            totals[g] = totals[g] * jnp.exp2((tops[g] - top) * EXP2) + part
        else:
            totals[g] = part
        tops[g] = top
        seen.add(g)
        return peaks

    def finish(g):
        total = totals[g]
        attn = (total[:DH, :] / total[DH : DH + 1, :]).astype(BF).astype(F32)
        square = jnp.sum(attn * attn, axis=0, keepdims=True)
        pieces = []
        for i in range(GROUP):
            cut = slice(i * ROWS, (i + 1) * ROWS)
            sqbuf[...] += jnp.broadcast_to(square[:, cut], (8, ROWS))
            gain = gain_ref[:, pl.ds((g * GROUP + i) * DH, DH)].astype(F32)
            pieces.append((attn[:, cut].T * gain).astype(BF))
        acc_out[...] += jnp.dot(
            jnp.concatenate(pieces, axis=1), w[pl.ds(g * TQ, TQ), :], preferred_element_type=F32
        )

    def largest(g, top):
        for i in range(GROUP):
            best = jnp.max(top[:, i * ROWS : (i + 1) * ROWS], axis=1, keepdims=True) * SCALE
            mxbuf[...] = jnp.where(mlane == g * GROUP + i, best, mxbuf[...])

    def buffer(n, tile):
        return s_buf.at[n % 2, pl.ds(0, SIZE[tile] * ROWS), :]

    def late(g, tile):
        return s_late.at[g, pl.ds((FIRST[tile] - FIRST[LATE]) * ROWS, SIZE[tile] * ROWS), :]

    groups = HEADS // GROUP
    steps = [i for i in SCHEDULE if isinstance(i[0], int)]
    seen = set()
    n = 0
    peak = None
    for k, item in enumerate(SCHEDULE):
        if item[0] == "arrive":
            t.arrive(*item[1:])
        if not isinstance(item[0], int):
            continue
        g, tile = item
        if peak is None:
            ready(g, tile)
            peak = score(g, tile, buffer(n, tile))
        ready_v(tile)
        ahead = []
        if n + 1 == len(steps):
            ready(0, LATE)
            ahead = [(0, LATE, late(0, LATE))]
        elif SCHEDULE[k + 1][0] != "flush":
            ready(*steps[n + 1])
            ahead = [(*steps[n + 1], buffer(n + 1, steps[n + 1][1]))]
        top = jnp.maximum(tops[g], peak) if g in seen else peak
        peaks = weigh(g, FIRST[tile], SIZE[tile], buffer(n, tile), top, ahead)
        peak = peaks[0] if peaks else None
        n += 1
    late_tops = [peak] + [score(g, LATE, late(g, LATE)) for g in range(1, groups)]
    t.sent()
    for g in range(groups):
        ready(g, LATE + 1)
        late_top = score(g, LATE + 1, late(g, LATE + 1))
        late_tops[g] = jnp.maximum(jnp.maximum(tops[g], late_tops[g]), late_top)
        largest(g, late_tops[g])
    for d in (1, 2, 3):
        t.add(("mx", d), mxbuf, mxgot.at[d], device(y, x + d, z, c))
        t.start(("mx", d))
    ready_v(LATE)
    ready_v(LATE + 1)
    wcopy.wait()
    for g in range(groups):
        weigh(g, FIRST[LATE], SLOTS - FIRST[LATE], s_late.at[g], late_tops[g])
        finish(g)
        if g == 2:
            t.arrive(*[("mx", d) for d in (1, 2, 3)])
            mx2[...] = jnp.maximum(jnp.maximum(mxbuf[...], mxgot[1]), jnp.maximum(mxgot[2], mxgot[3]))
            for d in range(NZ):
                t.add(("mz", d), mx2, mxgot2.at[d], device(y + 2, x, z + d, c))
                t.start(("mz", d))

    for j in range(4):
        parts[j] = acc_out[:, pl.ds(j * OUT, OUT)].astype(BF)
    for i, to in reversed(list(enumerate(mates))):
        t.add(("sq", i), sqbuf, sqgot.at[i], to)
        t.add(("rs", i), parts.at[to[2]], got.at[i], to)
        t.start(("sq", i))
        t.start(("rs", i))
    t.arrive(*[(a, i) for i in range(3) for a in ("sq", "rs")])
    square = sqbuf[...] + sqgot[0] + sqgot[1] + sqgot[2]
    inverse = lax.rsqrt(square * (1.0 / FEATURES) + 1e-05)
    inverse = jnp.broadcast_to(inverse[:1, :], (ROWS, ROWS)).T
    own = parts[tp].astype(F32)
    result = own + got[0].astype(F32) + got[1].astype(F32) + got[2].astype(F32)
    kv_out[...] = (result * jnp.concatenate([inverse, inverse], axis=1)).astype(BF)
    t.arrive(*[("mz", d) for d in range(NZ)])
    best = mxgot2[0]
    for d in range(1, NZ):
        best = jnp.maximum(best, mxgot2[d])
    max_out[...] = best[:1, :HEADS]
    t.sent()


def on_device(queries, key_vectors, value_vectors, block_order, norm_gain, kv_weight):
    any_ = pl.BlockSpec(memory_space=pl.ANY)
    vmem = pl.BlockSpec(memory_space=pltpu.VMEM)
    kv, peak = pl.pallas_call(
        kernel,
        out_shape=(jax.ShapeDtypeStruct((ROWS, OUT), BF), jax.ShapeDtypeStruct((1, HEADS), F32)),
        in_specs=[pl.BlockSpec(memory_space=pltpu.SMEM), vmem, any_, any_, any_, any_],
        out_specs=(vmem, vmem),
        scratch_shapes=[
            pltpu.VMEM((SLOTS * ROWS, 2 * DH), BF),
            pltpu.VMEM((SLOTS, VROWS, ROWS), BF),
            pltpu.VMEM((ROWS, DH), BF),
            pltpu.VMEM((DH, ROWS), BF),
            pltpu.VMEM((HEADS * ROWS, 2 * DH), BF),
            pltpu.VMEM((HEADS * DH, COLS), BF),
            pltpu.VMEM((2, TK, TQ), F32),
            pltpu.VMEM((HEADS // GROUP, (SLOTS - FIRST[LATE]) * ROWS, TQ), F32),
            pltpu.VMEM((HEADS // GROUP, 1, TQ), F32),
            pltpu.VMEM((HEADS // GROUP, VROWS, TQ), F32),
            pltpu.VMEM((ROWS, COLS), F32),
            pltpu.VMEM((4, ROWS, OUT), BF),
            pltpu.VMEM((3, ROWS, OUT), BF),
            pltpu.VMEM((8, DH), F32),
            pltpu.VMEM((3, 8, DH), F32),
            pltpu.VMEM((8, DH), F32),
            pltpu.VMEM((4, 8, DH), F32),
            pltpu.VMEM((8, DH), F32),
            pltpu.VMEM((NZ, 8, DH), F32),
            pltpu.SemaphoreType.DMA((N_SEM,)),
            pltpu.SemaphoreType.DMA((N_SEM,)),
            pltpu.SemaphoreType.DMA((2,)),
        ],
        compiler_params=pltpu.CompilerParams(
            collective_id=0, has_side_effects=True, vmem_limit_bytes=VMEM_LIMIT
        ),
        name="attention",
    )(
        block_order,
        norm_gain,
        queries[0],
        key_vectors[0],
        value_vectors[0],
        kv_weight[0],
    )
    return peak, kv[None]


def solution(mesh):
    return jax.shard_map(
        on_device,
        mesh=mesh,
        in_specs=(
            P("pp", "cp", "tp"),
            P("pp", "cp", "tp"),
            P("pp", "cp", "tp"),
            P(),
            P("pp", "tp"),
            P("pp", "tp", None),
        ),
        out_specs=(P("pp", "tp"), P("pp", "cp", "tp")),
        check_vma=False,
    )
```

```python
import math

import jax
import jax.numpy as jnp
from jax import lax
from jax.experimental import pallas as pl
from jax.experimental.pallas import tpu as pltpu
from jax.sharding import PartitionSpec as P

BF = jnp.bfloat16
F32 = jnp.float32
MESH = pl.DeviceIdType.MESH

DH = 128
ROWS = 128
HALF = 64
HEADS = 16
NX, NZ = 4, 8
SLOTS = NX * NZ
FEATURES = 8192
GROUP = 4
TQ = GROUP * ROWS
TK = 8 * ROWS
VROWS = 144
COLS = 1024
OUT = 256
BIG = 2.0**100
SCALE = 1.0 / math.sqrt(DH)
EXP2 = SCALE * math.log2(math.e)
N_SEM = 128
VMEM_LIMIT = 48 << 20
TILES = (
    [(0, dx) for dx in range(NX)],
    [(1, 0), (-1, 0), (2, 0), (-2, 0)],
    [(dz, dx) for dx in (1, 3, 2) for dz in (1, -1)],
    [(dz, dx) for dx in (1, 3, 2) for dz in (2, -2)],
    [(dz, dx) for dx in (0, 1, 3, 2) for dz in (3, -3)],
    [(4, dx) for dx in range(NX)],
)
SLOT = {(dz % NZ, dx): i for i, (dz, dx) in enumerate(sum(TILES, []))}
FIRST = [SLOT[t[0][0] % NZ, t[0][1]] for t in TILES]
SIZE = [len(t) for t in TILES]
LATE = 5


def ring(i, *dxs):
    return ("arrive", *[(a, i, dx) for dx in dxs for a in ("ku", "kd")])


SCHEDULE = (
    [("arrive", ("kx", 3), ("kx", 1), ("kx", 2))]
    + [("arrive", ("vz", 2), ("vz", -2), ("vz", 1), ("vz", -1)), ring(0, 0)]
    + [(0, 0), ("flush",), ("arrive", ("vz", 3), ("vz", -3), ("vz", 4), ("vz", -4))]
    + [ring(0, 1, 3, 2), ring(1, 0)]
    + [(1, 0), (0, 1), (1, 1), (2, 0), (2, 1), (0, 2), ring(1, 1, 3), (1, 2), ring(1, 2)]
    + [(2, 2), ring(2, 0), (3, 0), (3, 1), (3, 2), (0, 3), ring(2, 1, 3), (1, 3), ring(2, 2)]
    + [(2, 3), (3, 3), (0, 4), (1, 4), (2, 4), (3, 4), ("flush",)]
)


def slot_of(dz, dx):
    return SLOT[dz % NZ, dx % NX]


def device(y, x, z, c):
    return ((y % 4) // 2, (x % NX) * NZ + z % NZ, (y % 2) * 2 + c)


class Traffic:
    def __init__(self, send, recv):
        self.send, self.recv = send, recv
        self.copies = {}
        self.after = {}
        self.need = {}
        self.came = set()
        self.started = []

    def add(self, name, src, dst, to, after=()):
        i = len(self.copies)
        self.copies[name] = pltpu.make_async_remote_copy(
            src_ref=src,
            dst_ref=dst,
            send_sem=self.send.at[i],
            recv_sem=self.recv.at[i],
            device_id=to,
            device_id_type=MESH,
        )
        self.need[name] = set(after)
        for a in after:
            self.after.setdefault(a, []).append(name)

    def start(self, name):
        self.copies[name].start()
        self.started.append(name)

    def arrive(self, *names):
        for name in names:
            if name in self.came:
                continue
            self.came.add(name)
            self.copies[name].wait_recv()
            for child in self.after.get(name, ()):
                self.need[child].discard(name)
                if not self.need[child]:
                    self.start(child)

    def sent(self):
        for name in self.started:
            self.copies[name].wait_send()
        self.started = []


def kernel(
    order_hbm, gain_hbm, q_hbm, k_hbm, v_hbm, w_hbm,
    kv_out, max_out,
    order, gain_ref, kbuf, vt, vin, vown, qs, w, s_buf, s_late, tops, totals, acc_out, parts, got,
    sqbuf, sqgot, mxbuf, mxgot, mx2, mxgot2, send, recv, local,
):
    pp, cp, tp = lax.axis_index("pp"), lax.axis_index("cp"), lax.axis_index("tp")
    y, x, z, c = pp * 2 + tp // 2, cp // NZ, cp % NZ, tp % 2

    vcopy = pltpu.make_async_copy(v_hbm, vin, local.at[1])
    vcopy.start()
    ocopy = pltpu.make_async_copy(order_hbm, order, local.at[2])
    ocopy.start()
    gcopy = pltpu.make_async_copy(gain_hbm, gain_ref, local.at[3])
    gcopy.start()
    barrier = pltpu.get_barrier_semaphore()
    peers = [device(y, x + d, z, c) for d in (1, 2, 3)]
    peers += [device(y, x, z + d, c) for d in (1, 2, 6, 7)]
    peers += [device(y + 2, x, z + d, c) for d in range(NZ)]
    other = y // 2 * 2 + 1 - y % 2
    mates = [device(y, x, z, 1 - c), device(other, x, z, c), device(other, x, z, 1 - c)]
    for d in peers + mates:
        pl.semaphore_signal(barrier, inc=1, device_id=d, device_id_type=MESH)
    wcopy = pltpu.make_async_copy(w_hbm, w, local.at[0])
    wcopy.start()

    vcopy.wait()
    ocopy.wait()
    gcopy.wait()
    vown[...] = vin[...].astype(F32).T.astype(BF)

    t = Traffic(send, recv)

    def ks(dz, dx, lo=0, n=ROWS):
        return kbuf.at[pl.ds(slot_of(dz, dx) * ROWS + lo, n), pl.ds(0, DH)]

    def vs(dz, dx, lo=0, n=DH):
        return vt.at[slot_of(dz, dx), pl.ds(lo, n), :]

    partner = device(y + 2, x, z, c)
    t.add("k", k_hbm, ks(0, 0), partner)
    t.add("v", vown, vs(0, 0), partner)
    for h in range(HEADS):
        t.add(
            ("q", h),
            q_hbm.at[:, pl.ds(h * DH, DH)],
            qs.at[pl.ds(h * ROWS, ROWS), pl.ds(0, DH)],
            partner,
        )
    for d in (1, -1, 2, -2):
        t.add(("vz", d), vs(0, 0), vs(-d, 0), device(y, x, z + d, c), ["v"])
    for d in (1, 3, 2):
        t.add(("kx", d), ks(0, 0), ks(0, -d), device(y, x + d, z, c), ["k"])
    for d in (1, -1):
        lo = 0 if d > 0 else HALF
        far, near = device(y, x, z + 2 * d, c), device(y, x, z + d, c)
        t.add(("vz", 3 * d), vs(-2 * d, 0), vs(-3 * d, 0), near, [("vz", 2 * d)])
        t.add(("vz", 4 * d), vs(-2 * d, 0, lo, HALF), vs(4, 0, lo, HALF), far, [("vz", 2 * d)])
    for i in range(4):
        for dx in (0, 1, 3, 2):
            first = ["k"] if dx == 0 else [("kx", 4 - dx)]
            n, lo = (ROWS, 0) if i < 3 else (HALF, HALF)
            t.add(
                ("ku", i, dx), ks(-i, dx, 0, n), ks(-i - 1, dx, 0, n),
                device(y, x, z + 1, c), first if i == 0 else [("ku", i - 1, dx)],
            )
            t.add(
                ("kd", i, dx), ks(i, dx, lo, n), ks(i + 1, dx, lo, n),
                device(y, x, z - 1, c), first if i == 0 else [("kd", i - 1, dx)],
            )
    for dz in (0, 1, -1, 2, -2, 3, -3, 4):
        came = ["v"] if dz == 0 else [("vz", 4), ("vz", -4)] if dz == 4 else [("vz", -dz)]
        for d in (1, 3, 2):
            t.add(("vx", dz, d), vs(dz, 0), vs(dz, -d), device(y, x + d, z, c), came)

    pl.semaphore_wait(barrier, len(peers) + len(mates))

    for name in ["k", "v"] + [("q", h) for h in range(HEADS)]:
        t.start(name)

    row = lax.broadcasted_iota(jnp.int32, (ROWS, DH), 0)
    lane = lax.broadcasted_iota(jnp.int32, (ROWS, DH), 1)
    mine = (lane >= HALF) == (row >= HALF)
    off = lane % HALF
    q_mask = jnp.where(mine & ((off == 0) | (off > row % HALF)), -BIG, 0.0).astype(BF)
    for h in range(HEADS):
        qs[pl.ds(h * ROWS, ROWS), pl.ds(DH, DH)] = q_mask
    hrow = lax.broadcasted_iota(jnp.int32, (HALF, DH), 0)
    hlane = lax.broadcasted_iota(jnp.int32, (HALF, DH), 1)
    hoff = hlane % HALF
    after_all = (hoff == 0).astype(F32)
    in_block = ((hoff == hrow) & (hoff > 0)).astype(F32)
    half_id = jnp.where(hlane < HALF, order[2 * cp], order[2 * cp + 1])

    def masks(dz):
        for dx in range(NX):
            slot = slot_of(dz, dx)
            src = ((x + dx) % NX) * NZ + (z + dz) % NZ
            for b in range(2):
                block = order[2 * src + b]
                k_mask = jnp.where(half_id < block, after_all, jnp.where(half_id == block, in_block, 0.0))
                kbuf[pl.ds(slot * ROWS + b * HALF, HALF), pl.ds(DH, DH)] = k_mask.astype(BF)
            vt[slot, pl.ds(DH, VROWS - DH), :] = jnp.ones((VROWS - DH, ROWS), BF)

    for dz in range(NZ):
        masks(dz)
    acc_out[...] = jnp.zeros_like(acc_out)
    sqbuf[...] = jnp.zeros_like(sqbuf)
    mxbuf[...] = jnp.full_like(mxbuf, -BIG)
    mlane = lax.broadcasted_iota(jnp.int32, (8, DH), 1)
    t.arrive("k", "v")

    def score(g, tile, into):
        first, size = FIRST[tile] * ROWS, SIZE[tile] * ROWS
        s = lax.dot_general(
            kbuf[pl.ds(first, size), :], qs[pl.ds(g * TQ, TQ), :],
            (((1,), (1,)), ((), ())), preferred_element_type=F32,
        )
        into[...] = s
        return jnp.max(s, axis=0, keepdims=True)

    def ready(g, tile):
        t.arrive(*[("q", h) for h in range(g * GROUP, (g + 1) * GROUP)])
        for dz, dx in TILES[tile]:
            if dz == 0:
                t.arrive("k" if dx == 0 else ("kx", 4 - dx))
            elif dz == 4:
                t.arrive(("ku", 3, dx), ("kd", 3, dx))
            else:
                t.arrive(("kd" if dz > 0 else "ku", abs(dz) - 1, dx))

    def ready_v(tile):
        for dz, dx in TILES[tile]:
            t.arrive(*(["v"] if dz == 0 else [("vz", 4), ("vz", -4)] if dz == 4 else [("vz", -dz)]))
            if dx:
                t.arrive(("vx", dz, 4 - dx))

    def weigh(g, first, size, scores, top, ahead=()):
        p = jnp.exp2((scores[...] - top) * EXP2).astype(BF)
        peaks = [score(*a) for a in ahead]
        values = jnp.concatenate([vt[first + i] for i in range(size)], axis=1)
        part = jnp.dot(values, p, preferred_element_type=F32)
        if g in seen:
            totals[g] = totals[g] * jnp.exp2((tops[g] - top) * EXP2) + part
        else:
            totals[g] = part
        tops[g] = top
        seen.add(g)
        return peaks

    def finish(g):
        total = totals[g]
        attn = (total[:DH, :] / total[DH : DH + 1, :]).astype(BF).astype(F32)
        square = jnp.sum(attn * attn, axis=0, keepdims=True)
        pieces = []
        for i in range(GROUP):
            cut = slice(i * ROWS, (i + 1) * ROWS)
            sqbuf[...] += jnp.broadcast_to(square[:, cut], (8, ROWS))
            gain = gain_ref[:, pl.ds((g * GROUP + i) * DH, DH)].astype(F32)
            pieces.append((attn[:, cut].T * gain).astype(BF))
        acc_out[...] += jnp.dot(
            jnp.concatenate(pieces, axis=1), w[pl.ds(g * TQ, TQ), :], preferred_element_type=F32
        )

    def largest(g, top):
        for i in range(GROUP):
            best = jnp.max(top[:, i * ROWS : (i + 1) * ROWS], axis=1, keepdims=True) * SCALE
            mxbuf[...] = jnp.where(mlane == g * GROUP + i, best, mxbuf[...])

    def buffer(n, tile):
        return s_buf.at[n % 2, pl.ds(0, SIZE[tile] * ROWS), :]

    groups = HEADS // GROUP
    steps = [i for i in SCHEDULE if isinstance(i[0], int)]
    seen = set()
    n = 0
    peak = None
    for k, item in enumerate(SCHEDULE):
        if item[0] == "arrive":
            t.arrive(*item[1:])
        if not isinstance(item[0], int):
            continue
        g, tile = item
        if peak is None:
            ready(g, tile)
            peak = score(g, tile, buffer(n, tile))
        ready_v(tile)
        ahead = []
        if SCHEDULE[k + 1][0] != "flush":
            ready(*steps[n + 1])
            ahead = [(*steps[n + 1], buffer(n + 1, steps[n + 1][1]))]
        top = jnp.maximum(tops[g], peak) if g in seen else peak
        peaks = weigh(g, FIRST[tile], SIZE[tile], buffer(n, tile), top, ahead)
        peak = peaks[0] if peaks else None
        n += 1
    t.sent()
    late_tops = []
    for g in range(groups):
        ready(g, LATE)
        late_tops.append(jnp.maximum(tops[g], score(g, LATE, s_late.at[g])))
        largest(g, late_tops[g])
    for d in (1, 2, 3):
        t.add(("mx", d), mxbuf, mxgot.at[d], device(y, x + d, z, c))
        t.start(("mx", d))
    ready_v(LATE)
    wcopy.wait()
    for g in range(groups):
        weigh(g, FIRST[LATE], SIZE[LATE], s_late.at[g], late_tops[g])
        finish(g)
        if g == 2:
            t.arrive(*[("mx", d) for d in (1, 2, 3)])
            mx2[...] = jnp.maximum(jnp.maximum(mxbuf[...], mxgot[1]), jnp.maximum(mxgot[2], mxgot[3]))
            for d in range(NZ):
                t.add(("mz", d), mx2, mxgot2.at[d], device(y + 2, x, z + d, c))
                t.start(("mz", d))

    for j in range(4):
        parts[j] = acc_out[:, pl.ds(j * OUT, OUT)].astype(BF)
    for i, to in reversed(list(enumerate(mates))):
        t.add(("sq", i), sqbuf, sqgot.at[i], to)
        t.add(("rs", i), parts.at[to[2]], got.at[i], to)
        t.start(("sq", i))
        t.start(("rs", i))
    t.arrive(*[(a, i) for i in range(3) for a in ("sq", "rs")])
    square = sqbuf[...] + sqgot[0] + sqgot[1] + sqgot[2]
    inverse = lax.rsqrt(square * (1.0 / FEATURES) + 1e-05)
    inverse = jnp.broadcast_to(inverse[:1, :], (ROWS, ROWS)).T
    own = parts[tp].astype(F32)
    result = own + got[0].astype(F32) + got[1].astype(F32) + got[2].astype(F32)
    kv_out[...] = (result * jnp.concatenate([inverse, inverse], axis=1)).astype(BF)
    t.arrive(*[("mz", d) for d in range(NZ)])
    best = mxgot2[0]
    for d in range(1, NZ):
        best = jnp.maximum(best, mxgot2[d])
    max_out[...] = best[:1, :HEADS]
    t.sent()


def on_device(queries, key_vectors, value_vectors, block_order, norm_gain, kv_weight):
    hbm = pl.BlockSpec(memory_space=pltpu.HBM)
    vmem = pl.BlockSpec(memory_space=pltpu.VMEM)
    kv, peak = pl.pallas_call(
        kernel,
        out_shape=(jax.ShapeDtypeStruct((ROWS, OUT), BF), jax.ShapeDtypeStruct((1, HEADS), F32)),
        in_specs=[hbm] * 6,
        out_specs=(vmem, vmem),
        scratch_shapes=[
            pltpu.SMEM((2 * SLOTS,), jnp.int32),
            pltpu.VMEM((1, HEADS * DH), BF),
            pltpu.VMEM((SLOTS * ROWS, 2 * DH), BF),
            pltpu.VMEM((SLOTS, VROWS, ROWS), BF),
            pltpu.VMEM((ROWS, DH), BF),
            pltpu.VMEM((DH, ROWS), BF),
            pltpu.VMEM((HEADS * ROWS, 2 * DH), BF),
            pltpu.VMEM((HEADS * DH, COLS), BF),
            pltpu.VMEM((2, TK, TQ), F32),
            pltpu.VMEM((HEADS // GROUP, SIZE[LATE] * ROWS, TQ), F32),
            pltpu.VMEM((HEADS // GROUP, 1, TQ), F32),
            pltpu.VMEM((HEADS // GROUP, VROWS, TQ), F32),
            pltpu.VMEM((ROWS, COLS), F32),
            pltpu.VMEM((4, ROWS, OUT), BF),
            pltpu.VMEM((3, ROWS, OUT), BF),
            pltpu.VMEM((8, DH), F32),
            pltpu.VMEM((3, 8, DH), F32),
            pltpu.VMEM((8, DH), F32),
            pltpu.VMEM((4, 8, DH), F32),
            pltpu.VMEM((8, DH), F32),
            pltpu.VMEM((NZ, 8, DH), F32),
            pltpu.SemaphoreType.DMA((N_SEM,)),
            pltpu.SemaphoreType.DMA((N_SEM,)),
            pltpu.SemaphoreType.DMA((4,)),
        ],
        compiler_params=pltpu.CompilerParams(
            collective_id=0, has_side_effects=True, vmem_limit_bytes=VMEM_LIMIT
        ),
        name="attention",
    )(
        *[
            pltpu.with_memory_space_constraint(a, pltpu.HBM)
            for a in (block_order, norm_gain, queries[0], key_vectors[0], value_vectors[0], kv_weight[0])
        ]
    )
    return peak, kv[None]


def solution(mesh):
    return jax.shard_map(
        on_device,
        mesh=mesh,
        in_specs=(
            P("pp", "cp", "tp"),
            P("pp", "cp", "tp"),
            P("pp", "cp", "tp"),
            P(),
            P("pp", "tp"),
            P("pp", "tp", None),
        ),
        out_specs=(P("pp", "tp"), P("pp", "cp", "tp")),
        check_vma=False,
    )
```

```python
import math

import jax
import jax.numpy as jnp
from jax import lax
from jax.experimental import pallas as pl
from jax.experimental.pallas import tpu as pltpu
from jax.sharding import PartitionSpec as P

BF = jnp.bfloat16
F32 = jnp.float32
MESH = pl.DeviceIdType.MESH

DH = 128
ROWS = 128
HALF = 64
HEADS = 16
NX, NZ = 4, 8
SLOTS = NX * NZ
FEATURES = 8192
GROUP = 4
TQ = GROUP * ROWS
TK = 8 * ROWS
VROWS = 144
COLS = 1024
OUT = 256
BIG = 2.0**100
SCALE = 1.0 / math.sqrt(DH)
EXP2 = SCALE * math.log2(math.e)
N_SEM = 128
VMEM_LIMIT = 48 << 20
TILES = (
    [(0, dx) for dx in range(NX)],
    [(1, 0), (-1, 0), (2, 0), (-2, 0)],
    [(dz, dx) for dx in (1, 3, 2) for dz in (1, -1)],
    [(dz, dx) for dx in (1, 3, 2) for dz in (2, -2)] + [(3, 0), (-3, 0)],
    [(dz, dx) for dx in (1, 3, 2) for dz in (3, -3)] + [(4, 0)],
    [(4, dx) for dx in (1, 3, 2)],
)
SLOT = {(dz % NZ, dx): i for i, (dz, dx) in enumerate(sum(TILES, []))}
FIRST = [SLOT[t[0][0] % NZ, t[0][1]] for t in TILES]
SIZE = [len(t) for t in TILES]
LATE = 5


def ring(i, *dxs):
    return ("arrive", *[(a, i, dx) for dx in dxs for a in ("ku", "kd")])


SCHEDULE = (
    [("arrive", ("kx", 3), ("kx", 1), ("kx", 2))]
    + [("arrive", ("vz", 1), ("vz", -1)), ring(0, 0)]
    + [(0, 0), ("flush",), ring(0, 1, 3, 2), ("arrive", ("vz", 2), ("vz", -2)), ring(1, 0)]
    + [(1, 0), (0, 1), (1, 1), (2, 0), (2, 1), ("arrive", ("vz", 3), ("vz", -3))]
    + [(0, 2), ring(1, 1, 3), (1, 2), ring(1, 2)]
    + [(2, 2), ring(2, 0), (3, 0), (3, 1), ("arrive", ("vz", 4), ("vz", -4))]
    + [(3, 2), (0, 3), ring(2, 1, 3), (1, 3), ring(2, 2)]
    + [(2, 3), (3, 3), (0, 4), (1, 4), (2, 4), (3, 4), ("flush",)]
)


def slot_of(dz, dx):
    return SLOT[dz % NZ, dx % NX]


def device(y, x, z, c):
    return ((y % 4) // 2, (x % NX) * NZ + z % NZ, (y % 2) * 2 + c)


class Traffic:
    def __init__(self, send, recv):
        self.send, self.recv = send, recv
        self.copies = {}
        self.after = {}
        self.need = {}
        self.came = set()
        self.started = []

    def add(self, name, src, dst, to, after=()):
        i = len(self.copies)
        self.copies[name] = pltpu.make_async_remote_copy(
            src_ref=src,
            dst_ref=dst,
            send_sem=self.send.at[i],
            recv_sem=self.recv.at[i],
            device_id=to,
            device_id_type=MESH,
        )
        self.need[name] = set(after)
        for a in after:
            self.after.setdefault(a, []).append(name)

    def start(self, name):
        self.copies[name].start()
        self.started.append(name)

    def arrive(self, *names):
        for name in names:
            if name in self.came:
                continue
            self.came.add(name)
            self.copies[name].wait_recv()
            for child in self.after.get(name, ()):
                self.need[child].discard(name)
                if not self.need[child]:
                    self.start(child)

    def sent(self):
        for name in self.started:
            self.copies[name].wait_send()
        self.started = []


def kernel(
    order_hbm, gain_hbm, q_hbm, k_hbm, v_hbm, w_hbm,
    kv_out, max_out,
    order, gain_ref, kbuf, vt, vin, vown, qs, w, s_buf, s_late, tops, totals, acc_out, parts, got,
    sqbuf, sqgot, mxbuf, mxgot, mx2, mxgot2, send, recv, local,
):
    pp, cp, tp = lax.axis_index("pp"), lax.axis_index("cp"), lax.axis_index("tp")
    y, x, z, c = pp * 2 + tp // 2, cp // NZ, cp % NZ, tp % 2

    vcopy = pltpu.make_async_copy(v_hbm, vin, local.at[1])
    vcopy.start()
    ocopy = pltpu.make_async_copy(order_hbm, order, local.at[2])
    ocopy.start()
    gcopy = pltpu.make_async_copy(gain_hbm, gain_ref, local.at[3])
    gcopy.start()
    barrier = pltpu.get_barrier_semaphore()
    peers = [device(y, x + d, z, c) for d in (1, 2, 3)]
    peers += [device(y, x, z + d, c) for d in (1, 7)]
    peers += [device(y + 2, x, z + d, c) for d in range(NZ)]
    other = y // 2 * 2 + 1 - y % 2
    mates = [device(y, x, z, 1 - c), device(other, x, z, c), device(other, x, z, 1 - c)]
    for d in peers + mates:
        pl.semaphore_signal(barrier, inc=1, device_id=d, device_id_type=MESH)
    wcopy = pltpu.make_async_copy(w_hbm, w, local.at[0])
    wcopy.start()

    vcopy.wait()
    ocopy.wait()
    gcopy.wait()
    vown[...] = vin[...].astype(F32).T.astype(BF)

    t = Traffic(send, recv)

    def ks(dz, dx, lo=0, n=ROWS):
        return kbuf.at[pl.ds(slot_of(dz, dx) * ROWS + lo, n), pl.ds(0, DH)]

    def vs(dz, dx, lo=0, n=DH):
        return vt.at[slot_of(dz, dx), pl.ds(lo, n), :]

    partner = device(y + 2, x, z, c)
    t.add("k", k_hbm, ks(0, 0), partner)
    t.add("v", vown, vs(0, 0), partner)
    for h in range(HEADS):
        t.add(
            ("q", h),
            q_hbm.at[:, pl.ds(h * DH, DH)],
            qs.at[pl.ds(h * ROWS, ROWS), pl.ds(0, DH)],
            partner,
        )
    for d in (1, -1):
        near = device(y, x, z + d, c)
        for i in range(4):
            n, lo = (DH, 0) if i < 3 else (HALF, 0 if d > 0 else HALF)
            src, dst = vs(-i * d, 0, lo, n), vs(-(i + 1) * d, 0, lo, n)
            t.add(("vz", (i + 1) * d), src, dst, near, [("vz", i * d)] if i else ["v"])
    for d in (1, 3, 2):
        t.add(("kx", d), ks(0, 0), ks(0, -d), device(y, x + d, z, c), ["k"])
    for i in range(4):
        for dx in (0, 1, 3, 2):
            first = ["k"] if dx == 0 else [("kx", 4 - dx)]
            n, lo = (ROWS, 0) if i < 3 else (HALF, HALF)
            t.add(
                ("ku", i, dx), ks(-i, dx, 0, n), ks(-i - 1, dx, 0, n),
                device(y, x, z + 1, c), first if i == 0 else [("ku", i - 1, dx)],
            )
            t.add(
                ("kd", i, dx), ks(i, dx, lo, n), ks(i + 1, dx, lo, n),
                device(y, x, z - 1, c), first if i == 0 else [("kd", i - 1, dx)],
            )
    for dz in (0, 1, -1, 2, -2, 3, -3, 4):
        came = ["v"] if dz == 0 else [("vz", 4), ("vz", -4)] if dz == 4 else [("vz", -dz)]
        for d in (1, 3, 2):
            t.add(("vx", dz, d), vs(dz, 0), vs(dz, -d), device(y, x + d, z, c), came)

    pl.semaphore_wait(barrier, len(peers) + len(mates))

    for name in ["k", "v"] + [("q", h) for h in range(HEADS)]:
        t.start(name)

    row = lax.broadcasted_iota(jnp.int32, (ROWS, DH), 0)
    lane = lax.broadcasted_iota(jnp.int32, (ROWS, DH), 1)
    mine = (lane >= HALF) == (row >= HALF)
    off = lane % HALF
    q_mask = jnp.where(mine & ((off == 0) | (off > row % HALF)), -BIG, 0.0).astype(BF)
    for h in range(HEADS):
        qs[pl.ds(h * ROWS, ROWS), pl.ds(DH, DH)] = q_mask
    hrow = lax.broadcasted_iota(jnp.int32, (HALF, DH), 0)
    hlane = lax.broadcasted_iota(jnp.int32, (HALF, DH), 1)
    hoff = hlane % HALF
    after_all = (hoff == 0).astype(F32)
    in_block = ((hoff == hrow) & (hoff > 0)).astype(F32)
    half_id = jnp.where(hlane < HALF, order[2 * cp], order[2 * cp + 1])

    def masks(dz):
        for dx in range(NX):
            slot = slot_of(dz, dx)
            src = ((x + dx) % NX) * NZ + (z + dz) % NZ
            for b in range(2):
                block = order[2 * src + b]
                k_mask = jnp.where(half_id < block, after_all, jnp.where(half_id == block, in_block, 0.0))
                kbuf[pl.ds(slot * ROWS + b * HALF, HALF), pl.ds(DH, DH)] = k_mask.astype(BF)
            vt[slot, pl.ds(DH, VROWS - DH), :] = jnp.ones((VROWS - DH, ROWS), BF)

    for dz in range(NZ):
        masks(dz)
    sqbuf[...] = jnp.zeros_like(sqbuf)
    mxbuf[...] = jnp.full_like(mxbuf, -BIG)
    mlane = lax.broadcasted_iota(jnp.int32, (8, DH), 1)
    t.arrive("k", "v")

    def score(g, tile, into):
        first, size = FIRST[tile] * ROWS, SIZE[tile] * ROWS
        s = lax.dot_general(
            kbuf[pl.ds(first, size), :], qs[pl.ds(g * TQ, TQ), :],
            (((1,), (1,)), ((), ())), preferred_element_type=F32,
        )
        into[...] = s
        return jnp.max(s, axis=0, keepdims=True)

    def ready(g, tile):
        t.arrive(*[("q", h) for h in range(g * GROUP, (g + 1) * GROUP)])
        for dz, dx in TILES[tile]:
            if dz == 0:
                t.arrive("k" if dx == 0 else ("kx", 4 - dx))
            elif dz == 4:
                t.arrive(("ku", 3, dx), ("kd", 3, dx))
            else:
                t.arrive(("kd" if dz > 0 else "ku", abs(dz) - 1, dx))

    def ready_v(tile):
        for dz, dx in TILES[tile]:
            t.arrive(*(["v"] if dz == 0 else [("vz", 4), ("vz", -4)] if dz == 4 else [("vz", -dz)]))
            if dx:
                t.arrive(("vx", dz, 4 - dx))

    def weigh(g, first, size, scores, top, ahead=()):
        p = jnp.exp2((scores[...] - top) * EXP2).astype(BF)
        peaks = [score(*a) for a in ahead]
        values = jnp.concatenate([vt[first + i] for i in range(size)], axis=1)
        part = jnp.dot(values, p, preferred_element_type=F32)
        if g in seen:
            totals[g] = totals[g] * jnp.exp2((tops[g] - top) * EXP2) + part
        else:
            totals[g] = part
        tops[g] = top
        seen.add(g)
        return peaks

    def finish(g):
        total = totals[g]
        attn = (total[:DH, :] * (1.0 / total[DH : DH + 1, :])).astype(BF).astype(F32)
        square = jnp.sum(attn * attn, axis=0, keepdims=True)
        pieces = []
        for i in range(GROUP):
            cut = slice(i * ROWS, (i + 1) * ROWS)
            sqbuf[...] += jnp.broadcast_to(square[:, cut], (8, ROWS))
            gain = gain_ref[:, pl.ds((g * GROUP + i) * DH, DH)].astype(F32)
            pieces.append((attn[:, cut].T * gain).astype(BF))
        product = jnp.dot(
            jnp.concatenate(pieces, axis=1), w[pl.ds(g * TQ, TQ), :], preferred_element_type=F32
        )
        if g == 0:
            acc_out[...] = product
        elif g < groups - 1:
            acc_out[...] += product
        else:
            for j in range(4):
                cut = slice(j * OUT, (j + 1) * OUT)
                parts[j] = (acc_out[:, cut] + product[:, cut]).astype(BF)

    def largest(g, top):
        for i in range(GROUP):
            best = jnp.max(top[:, i * ROWS : (i + 1) * ROWS], axis=1, keepdims=True) * SCALE
            mxbuf[...] = jnp.where(mlane == g * GROUP + i, best, mxbuf[...])

    def buffer(n, tile):
        return s_buf.at[n % 2, pl.ds(0, SIZE[tile] * ROWS), :]

    groups = HEADS // GROUP
    steps = [i for i in SCHEDULE if isinstance(i[0], int)]
    seen = set()
    n = 0
    peak = None
    for k, item in enumerate(SCHEDULE):
        if item[0] == "arrive":
            t.arrive(*item[1:])
        if not isinstance(item[0], int):
            continue
        g, tile = item
        if peak is None:
            ready(g, tile)
            peak = score(g, tile, buffer(n, tile))
        ready_v(tile)
        ahead = []
        if SCHEDULE[k + 1][0] != "flush":
            ready(*steps[n + 1])
            ahead = [(*steps[n + 1], buffer(n + 1, steps[n + 1][1]))]
        top = jnp.maximum(tops[g], peak) if g in seen else peak
        peaks = weigh(g, FIRST[tile], SIZE[tile], buffer(n, tile), top, ahead)
        peak = peaks[0] if peaks else None
        n += 1
    t.sent()
    late_tops = []
    for g in range(groups):
        ready(g, LATE)
        late_tops.append(jnp.maximum(tops[g], score(g, LATE, s_late.at[g])))
        largest(g, late_tops[g])
    for d in (1, 2, 3):
        t.add(("mx", d), mxbuf, mxgot.at[d], device(y, x + d, z, c))
        t.start(("mx", d))
    ready_v(LATE)
    wcopy.wait()
    for g in range(groups):
        weigh(g, FIRST[LATE], SIZE[LATE], s_late.at[g], late_tops[g])
        finish(g)

    for i, to in reversed(list(enumerate(mates))):
        t.add(("sq", i), sqbuf, sqgot.at[i], to)
        t.add(("rs", i), parts.at[to[2]], got.at[i], to)
        t.start(("sq", i))
        t.start(("rs", i))
    t.arrive(*[("mx", d) for d in (1, 2, 3)])
    mx2[...] = jnp.maximum(jnp.maximum(mxbuf[...], mxgot[1]), jnp.maximum(mxgot[2], mxgot[3]))
    for d in range(NZ):
        t.add(("mz", d), mx2, mxgot2.at[d], device(y + 2, x, z + d, c))
        t.start(("mz", d))
    t.arrive(*[(a, i) for i in range(3) for a in ("sq", "rs")])
    square = sqbuf[...] + sqgot[0] + sqgot[1] + sqgot[2]
    inverse = lax.rsqrt(square * (1.0 / FEATURES) + 1e-05)
    inverse = jnp.broadcast_to(inverse[:1, :], (ROWS, ROWS)).T
    own = parts[tp].astype(F32)
    result = own + got[0].astype(F32) + got[1].astype(F32) + got[2].astype(F32)
    kv_out[...] = (result * jnp.concatenate([inverse, inverse], axis=1)).astype(BF)
    t.arrive(*[("mz", d) for d in range(NZ)])
    best = mxgot2[0]
    for d in range(1, NZ):
        best = jnp.maximum(best, mxgot2[d])
    max_out[...] = best[:1, :HEADS]
    t.sent()


def on_device(queries, key_vectors, value_vectors, block_order, norm_gain, kv_weight):
    hbm = pl.BlockSpec(memory_space=pltpu.HBM)
    vmem = pl.BlockSpec(memory_space=pltpu.VMEM)
    kv, peak = pl.pallas_call(
        kernel,
        out_shape=(jax.ShapeDtypeStruct((ROWS, OUT), BF), jax.ShapeDtypeStruct((1, HEADS), F32)),
        in_specs=[hbm] * 6,
        out_specs=(vmem, vmem),
        scratch_shapes=[
            pltpu.SMEM((2 * SLOTS,), jnp.int32),
            pltpu.VMEM((1, HEADS * DH), BF),
            pltpu.VMEM((SLOTS * ROWS, 2 * DH), BF),
            pltpu.VMEM((SLOTS, VROWS, ROWS), BF),
            pltpu.VMEM((ROWS, DH), BF),
            pltpu.VMEM((DH, ROWS), BF),
            pltpu.VMEM((HEADS * ROWS, 2 * DH), BF),
            pltpu.VMEM((HEADS * DH, COLS), BF),
            pltpu.VMEM((2, TK, TQ), F32),
            pltpu.VMEM((HEADS // GROUP, SIZE[LATE] * ROWS, TQ), F32),
            pltpu.VMEM((HEADS // GROUP, 1, TQ), F32),
            pltpu.VMEM((HEADS // GROUP, VROWS, TQ), F32),
            pltpu.VMEM((ROWS, COLS), F32),
            pltpu.VMEM((4, ROWS, OUT), BF),
            pltpu.VMEM((3, ROWS, OUT), BF),
            pltpu.VMEM((8, DH), F32),
            pltpu.VMEM((3, 8, DH), F32),
            pltpu.VMEM((8, DH), F32),
            pltpu.VMEM((4, 8, DH), F32),
            pltpu.VMEM((8, DH), F32),
            pltpu.VMEM((NZ, 8, DH), F32),
            pltpu.SemaphoreType.DMA((N_SEM,)),
            pltpu.SemaphoreType.DMA((N_SEM,)),
            pltpu.SemaphoreType.DMA((4,)),
        ],
        compiler_params=pltpu.CompilerParams(
            collective_id=0, has_side_effects=True, vmem_limit_bytes=VMEM_LIMIT
        ),
        name="attention",
    )(
        *[
            pltpu.with_memory_space_constraint(a, pltpu.HBM)
            for a in (block_order, norm_gain, queries[0], key_vectors[0], value_vectors[0], kv_weight[0])
        ]
    )
    return peak, kv[None]


def solution(mesh):
    return jax.shard_map(
        on_device,
        mesh=mesh,
        in_specs=(
            P("pp", "cp", "tp"),
            P("pp", "cp", "tp"),
            P("pp", "cp", "tp"),
            P(),
            P("pp", "tp"),
            P("pp", "tp", None),
        ),
        out_specs=(P("pp", "tp"), P("pp", "cp", "tp")),
        check_vma=False,
    )
```

```python
import math

import jax
import jax.numpy as jnp
from jax import lax
from jax.experimental import pallas as pl
from jax.experimental.pallas import tpu as pltpu
from jax.sharding import PartitionSpec as P

BF = jnp.bfloat16
F32 = jnp.float32
MESH = pl.DeviceIdType.MESH

DH = 128
ROWS = 128
HALF = 64
HEADS = 16
NX, NZ = 4, 8
SLOTS = NX * NZ
FEATURES = 8192
GROUP = 4
TQ = GROUP * ROWS
TK = 8 * ROWS
VROWS = 144
COLS = 1024
OUT = 256
BIG = 2.0**100
SCALE = 1.0 / math.sqrt(DH)
EXP2 = SCALE * math.log2(math.e)
N_SEM = 128
VMEM_LIMIT = 48 << 20
TILES = (
    [(0, dx) for dx in range(NX)],
    [(1, 0), (-1, 0), (2, 0), (-2, 0)],
    [(dz, dx) for dx in (1, 3, 2) for dz in (1, -1)],
    [(dz, dx) for dx in (1, 3, 2) for dz in (2, -2)] + [(3, 0), (-3, 0)],
    [(dz, dx) for dx in (1, 3, 2) for dz in (3, -3)] + [(4, 0)],
    [(4, dx) for dx in (1, 3, 2)],
)
SLOT = {(dz % NZ, dx): i for i, (dz, dx) in enumerate(sum(TILES, []))}
FIRST = [SLOT[t[0][0] % NZ, t[0][1]] for t in TILES]
SIZE = [len(t) for t in TILES]
LATE = 5


def ring(i, *dxs):
    return ("arrive", *[(a, i, dx) for dx in dxs for a in ("ku", "kd")])


SCHEDULE = (
    [("arrive", ("kx", 3), ("kx", 1), ("kx", 2))]
    + [("arrive", ("vz", 1), ("vz", -1)), ring(0, 0)]
    + [(0, 0), ("flush",), ring(0, 1, 3, 2), ("arrive", ("vz", 2), ("vz", -2)), ring(1, 0)]
    + [(1, 0), (0, 1), (1, 1), (2, 0), (2, 1), ("arrive", ("vz", 3), ("vz", -3))]
    + [(0, 2), ring(1, 1, 3), (1, 2), ring(1, 2)]
    + [(2, 2), ring(2, 0), (3, 0), (3, 1), ("arrive", ("vz", 4), ("vz", -4))]
    + [(3, 2), (0, 3), ring(2, 1, 3), (1, 3), ring(2, 2)]
    + [(2, 3), (3, 3), (0, 4), (1, 4), (2, 4), (3, 4), ("flush",)]
)


def slot_of(dz, dx):
    return SLOT[dz % NZ, dx % NX]


def device(y, x, z, c):
    return ((y % 4) // 2, (x % NX) * NZ + z % NZ, (y % 2) * 2 + c)


class Traffic:
    def __init__(self, send, recv):
        self.send, self.recv = send, recv
        self.copies = {}
        self.after = {}
        self.need = {}
        self.came = set()
        self.started = []

    def add(self, name, src, dst, to, after=()):
        i = len(self.copies)
        self.copies[name] = pltpu.make_async_remote_copy(
            src_ref=src,
            dst_ref=dst,
            send_sem=self.send.at[i],
            recv_sem=self.recv.at[i],
            device_id=to,
            device_id_type=MESH,
        )
        self.need[name] = set(after)
        for a in after:
            self.after.setdefault(a, []).append(name)

    def start(self, name):
        self.copies[name].start()
        self.started.append(name)

    def arrive(self, *names):
        for name in names:
            if name in self.came:
                continue
            self.came.add(name)
            self.copies[name].wait_recv()
            for child in self.after.get(name, ()):
                self.need[child].discard(name)
                if not self.need[child]:
                    self.start(child)

    def sent(self):
        for name in self.started:
            self.copies[name].wait_send()
        self.started = []


def kernel(
    order_hbm, gain_hbm, q_hbm, k_hbm, v_hbm, w_hbm,
    kv_out, max_out,
    order, gain_ref, kbuf, vt, vin, vown, qs, w, s_buf, s_late, tops, totals, acc_out, parts, got,
    sqbuf, sqgot, mxbuf, mxgot, mx2, mxgot2, send, recv, local,
):
    pp, cp, tp = lax.axis_index("pp"), lax.axis_index("cp"), lax.axis_index("tp")
    y, x, z, c = pp * 2 + tp // 2, cp // NZ, cp % NZ, tp % 2

    vcopy = pltpu.make_async_copy(v_hbm, vin, local.at[1])
    vcopy.start()
    ocopy = pltpu.make_async_copy(order_hbm, order, local.at[2])
    ocopy.start()
    gcopy = pltpu.make_async_copy(gain_hbm, gain_ref, local.at[3])
    gcopy.start()
    barrier = pltpu.get_barrier_semaphore()
    peers = [device(y, x + d, z, c) for d in (1, 2, 3)]
    peers += [device(y, x, z + d, c) for d in (1, 7)]
    peers += [device(y + 2, x, z + d, c) for d in range(NZ)]
    other = y // 2 * 2 + 1 - y % 2
    mates = [device(y, x, z, 1 - c), device(other, x, z, c), device(other, x, z, 1 - c)]
    for d in peers + mates:
        pl.semaphore_signal(barrier, inc=1, device_id=d, device_id_type=MESH)
    wcopy = pltpu.make_async_copy(w_hbm, w, local.at[0])
    wcopy.start()

    vcopy.wait()
    ocopy.wait()
    gcopy.wait()
    vown[...] = vin[...].astype(F32).T.astype(BF)

    t = Traffic(send, recv)

    def ks(dz, dx, lo=0, n=ROWS):
        return kbuf.at[pl.ds(slot_of(dz, dx) * ROWS + lo, n), pl.ds(0, DH)]

    def vs(dz, dx, lo=0, n=DH):
        return vt.at[slot_of(dz, dx), pl.ds(lo, n), :]

    partner = device(y + 2, x, z, c)
    t.add("k", k_hbm, ks(0, 0), partner)
    t.add("v", vown, vs(0, 0), partner)
    for h in range(HEADS):
        t.add(
            ("q", h),
            q_hbm.at[:, pl.ds(h * DH, DH)],
            qs.at[pl.ds(h * ROWS, ROWS), pl.ds(0, DH)],
            partner,
        )
    for d in (1, -1):
        near = device(y, x, z + d, c)
        for i in range(4):
            n, lo = (DH, 0) if i < 3 else (HALF, 0 if d > 0 else HALF)
            src, dst = vs(-i * d, 0, lo, n), vs(-(i + 1) * d, 0, lo, n)
            t.add(("vz", (i + 1) * d), src, dst, near, [("vz", i * d)] if i else ["v"])
    for d in (1, 3, 2):
        t.add(("kx", d), ks(0, 0), ks(0, -d), device(y, x + d, z, c), ["k"])
    for i in range(4):
        for dx in (0, 1, 3, 2):
            first = ["k"] if dx == 0 else [("kx", 4 - dx)]
            n, lo = (ROWS, 0) if i < 3 else (HALF, HALF)
            t.add(
                ("ku", i, dx), ks(-i, dx, 0, n), ks(-i - 1, dx, 0, n),
                device(y, x, z + 1, c), first if i == 0 else [("ku", i - 1, dx)],
            )
            t.add(
                ("kd", i, dx), ks(i, dx, lo, n), ks(i + 1, dx, lo, n),
                device(y, x, z - 1, c), first if i == 0 else [("kd", i - 1, dx)],
            )
    for dz in (0, 1, -1, 2, -2, 3, -3, 4):
        came = ["v"] if dz == 0 else [("vz", 4), ("vz", -4)] if dz == 4 else [("vz", -dz)]
        for d in (1, 3, 2):
            t.add(("vx", dz, d), vs(dz, 0), vs(dz, -d), device(y, x + d, z, c), came)

    pl.semaphore_wait(barrier, len(peers) + len(mates))

    for name in ["k", "v"] + [("q", h) for h in range(HEADS)]:
        t.start(name)

    row = lax.broadcasted_iota(jnp.int32, (ROWS, DH), 0)
    lane = lax.broadcasted_iota(jnp.int32, (ROWS, DH), 1)
    mine = (lane >= HALF) == (row >= HALF)
    off = lane % HALF
    q_mask = jnp.where(mine & ((off == 0) | (off > row % HALF)), -BIG, 0.0).astype(BF)
    for h in range(HEADS):
        qs[pl.ds(h * ROWS, ROWS), pl.ds(DH, DH)] = q_mask
    hrow = lax.broadcasted_iota(jnp.int32, (HALF, DH), 0)
    hlane = lax.broadcasted_iota(jnp.int32, (HALF, DH), 1)
    hoff = hlane % HALF
    after_all = (hoff == 0).astype(F32)
    in_block = ((hoff == hrow) & (hoff > 0)).astype(F32)
    half_id = jnp.where(hlane < HALF, order[2 * cp], order[2 * cp + 1])

    def masks(dz):
        for dx in range(NX):
            slot = slot_of(dz, dx)
            src = ((x + dx) % NX) * NZ + (z + dz) % NZ
            for b in range(2):
                block = order[2 * src + b]
                k_mask = jnp.where(half_id < block, after_all, jnp.where(half_id == block, in_block, 0.0))
                kbuf[pl.ds(slot * ROWS + b * HALF, HALF), pl.ds(DH, DH)] = k_mask.astype(BF)
            vt[slot, pl.ds(DH, VROWS - DH), :] = jnp.ones((VROWS - DH, ROWS), BF)

    for dz in range(NZ):
        masks(dz)
    sqbuf[...] = jnp.zeros_like(sqbuf)
    mxbuf[...] = jnp.full_like(mxbuf, -BIG)
    mlane = lax.broadcasted_iota(jnp.int32, (8, DH), 1)
    t.arrive("k", "v")

    def score(g, tile, into):
        first, size = FIRST[tile] * ROWS, SIZE[tile] * ROWS
        s = lax.dot_general(
            kbuf[pl.ds(first, size), :], qs[pl.ds(g * TQ, TQ), :],
            (((1,), (1,)), ((), ())), preferred_element_type=F32,
        )
        into[...] = s
        return jnp.max(s, axis=0, keepdims=True)

    def ready(g, tile):
        t.arrive(*[("q", h) for h in range(g * GROUP, (g + 1) * GROUP)])
        for dz, dx in TILES[tile]:
            if dz == 0:
                t.arrive("k" if dx == 0 else ("kx", 4 - dx))
            elif dz == 4:
                t.arrive(("ku", 3, dx), ("kd", 3, dx))
            else:
                t.arrive(("kd" if dz > 0 else "ku", abs(dz) - 1, dx))

    def ready_v(tile):
        for dz, dx in TILES[tile]:
            t.arrive(*(["v"] if dz == 0 else [("vz", 4), ("vz", -4)] if dz == 4 else [("vz", -dz)]))
            if dx:
                t.arrive(("vx", dz, 4 - dx))

    def weigh(g, first, size, scores, top, ahead=()):
        p = jnp.exp2((scores[...] - top) * EXP2).astype(BF)
        peaks = [score(*a) for a in ahead]
        values = jnp.concatenate([vt[first + i] for i in range(size)], axis=1)
        part = jnp.dot(values, p, preferred_element_type=F32)
        if g in seen:
            totals[g] = totals[g] * jnp.exp2((tops[g] - top) * EXP2) + part
        else:
            totals[g] = part
        tops[g] = top
        seen.add(g)
        return peaks

    def finish(g):
        total = totals[g]
        attn = (total[:DH, :] * (1.0 / total[DH : DH + 1, :])).astype(BF).astype(F32)
        square = jnp.sum(attn * attn, axis=0, keepdims=True)
        pieces = []
        for i in range(GROUP):
            cut = slice(i * ROWS, (i + 1) * ROWS)
            sqbuf[...] += jnp.broadcast_to(square[:, cut], (8, ROWS))
            gain = gain_ref[:, pl.ds((g * GROUP + i) * DH, DH)].astype(F32)
            pieces.append((attn[:, cut].T * gain).astype(BF))
        normed = jnp.concatenate(pieces, axis=1)
        if g < groups - 1:
            product = jnp.dot(normed, w[pl.ds(g * TQ, TQ), :], preferred_element_type=F32)
            acc_out[...] = product if g == 0 else acc_out[...] + product
            return
        for i, to in reversed(list(enumerate(mates))):
            t.add(("sq", i), sqbuf, sqgot.at[i], to)
            t.start(("sq", i))
        for i, dest in ((2, mates[2][2]), (1, mates[1][2]), (0, mates[0][2]), (3, tp)):
            cut = pl.ds(pl.multiple_of(dest * OUT, OUT), OUT)
            product = jnp.dot(normed, w[pl.ds(g * TQ, TQ), cut], preferred_element_type=F32)
            if i == 3:
                acc_out[:, cut] = acc_out[:, cut] + product
                return
            parts[i] = (acc_out[:, cut] + product).astype(BF)
            t.add(("rs", i), parts.at[i], got.at[i], mates[i])
            t.start(("rs", i))

    def largest(g, top):
        for i in range(GROUP):
            best = jnp.max(top[:, i * ROWS : (i + 1) * ROWS], axis=1, keepdims=True) * SCALE
            mxbuf[...] = jnp.where(mlane == g * GROUP + i, best, mxbuf[...])

    def buffer(n, tile):
        return s_buf.at[n % 2, pl.ds(0, SIZE[tile] * ROWS), :]

    groups = HEADS // GROUP
    steps = [i for i in SCHEDULE if isinstance(i[0], int)]
    seen = set()
    n = 0
    peak = None
    for k, item in enumerate(SCHEDULE):
        if item[0] == "arrive":
            t.arrive(*item[1:])
        if not isinstance(item[0], int):
            continue
        g, tile = item
        if peak is None:
            ready(g, tile)
            peak = score(g, tile, buffer(n, tile))
        ready_v(tile)
        ahead = []
        if SCHEDULE[k + 1][0] != "flush":
            ready(*steps[n + 1])
            ahead = [(*steps[n + 1], buffer(n + 1, steps[n + 1][1]))]
        top = jnp.maximum(tops[g], peak) if g in seen else peak
        peaks = weigh(g, FIRST[tile], SIZE[tile], buffer(n, tile), top, ahead)
        peak = peaks[0] if peaks else None
        n += 1
    late_tops = []
    for g in range(groups):
        ready(g, LATE)
        late_tops.append(jnp.maximum(tops[g], score(g, LATE, s_late.at[g])))
        largest(g, late_tops[g])
    for d in (1, 2, 3):
        t.add(("mx", d), mxbuf, mxgot.at[d], device(y, x + d, z, c))
        t.start(("mx", d))
    ready_v(LATE)
    wcopy.wait()
    for g in range(groups):
        weigh(g, FIRST[LATE], SIZE[LATE], s_late.at[g], late_tops[g])
        finish(g)

    t.arrive(*[("mx", d) for d in (1, 2, 3)])
    mx2[...] = jnp.maximum(jnp.maximum(mxbuf[...], mxgot[1]), jnp.maximum(mxgot[2], mxgot[3]))
    for d in range(NZ):
        t.add(("mz", d), mx2, mxgot2.at[d], device(y + 2, x, z + d, c))
        t.start(("mz", d))
    t.sent()
    t.arrive(*[(a, i) for i in range(3) for a in ("sq", "rs")])
    square = sqbuf[...] + sqgot[0] + sqgot[1] + sqgot[2]
    inverse = lax.rsqrt(square * (1.0 / FEATURES) + 1e-05)
    inverse = jnp.broadcast_to(inverse[:1, :], (ROWS, ROWS)).T
    own = acc_out[:, pl.ds(pl.multiple_of(tp * OUT, OUT), OUT)]
    result = own + got[0].astype(F32) + got[1].astype(F32) + got[2].astype(F32)
    kv_out[...] = (result * jnp.concatenate([inverse, inverse], axis=1)).astype(BF)
    t.arrive(*[("mz", d) for d in range(NZ)])
    best = mxgot2[0]
    for d in range(1, NZ):
        best = jnp.maximum(best, mxgot2[d])
    max_out[...] = best[:1, :HEADS]


def on_device(queries, key_vectors, value_vectors, block_order, norm_gain, kv_weight):
    hbm = pl.BlockSpec(memory_space=pltpu.HBM)
    vmem = pl.BlockSpec(memory_space=pltpu.VMEM)
    kv, peak = pl.pallas_call(
        kernel,
        out_shape=(jax.ShapeDtypeStruct((ROWS, OUT), BF), jax.ShapeDtypeStruct((1, HEADS), F32)),
        in_specs=[hbm] * 6,
        out_specs=(vmem, vmem),
        scratch_shapes=[
            pltpu.SMEM((2 * SLOTS,), jnp.int32),
            pltpu.VMEM((1, HEADS * DH), BF),
            pltpu.VMEM((SLOTS * ROWS, 2 * DH), BF),
            pltpu.VMEM((SLOTS, VROWS, ROWS), BF),
            pltpu.VMEM((ROWS, DH), BF),
            pltpu.VMEM((DH, ROWS), BF),
            pltpu.VMEM((HEADS * ROWS, 2 * DH), BF),
            pltpu.VMEM((HEADS * DH, COLS), BF),
            pltpu.VMEM((2, TK, TQ), F32),
            pltpu.VMEM((HEADS // GROUP, SIZE[LATE] * ROWS, TQ), F32),
            pltpu.VMEM((HEADS // GROUP, 1, TQ), F32),
            pltpu.VMEM((HEADS // GROUP, VROWS, TQ), F32),
            pltpu.VMEM((ROWS, COLS), F32),
            pltpu.VMEM((3, ROWS, OUT), BF),
            pltpu.VMEM((3, ROWS, OUT), BF),
            pltpu.VMEM((8, DH), F32),
            pltpu.VMEM((3, 8, DH), F32),
            pltpu.VMEM((8, DH), F32),
            pltpu.VMEM((4, 8, DH), F32),
            pltpu.VMEM((8, DH), F32),
            pltpu.VMEM((NZ, 8, DH), F32),
            pltpu.SemaphoreType.DMA((N_SEM,)),
            pltpu.SemaphoreType.DMA((N_SEM,)),
            pltpu.SemaphoreType.DMA((4,)),
        ],
        compiler_params=pltpu.CompilerParams(
            collective_id=0, has_side_effects=True, vmem_limit_bytes=VMEM_LIMIT
        ),
        name="attention",
    )(
        *[
            pltpu.with_memory_space_constraint(a, pltpu.HBM)
            for a in (block_order, norm_gain, queries[0], key_vectors[0], value_vectors[0], kv_weight[0])
        ]
    )
    return peak, kv[None]


def solution(mesh):
    return jax.shard_map(
        on_device,
        mesh=mesh,
        in_specs=(
            P("pp", "cp", "tp"),
            P("pp", "cp", "tp"),
            P("pp", "cp", "tp"),
            P(),
            P("pp", "tp"),
            P("pp", "tp", None),
        ),
        out_specs=(P("pp", "tp"), P("pp", "cp", "tp")),
        check_vma=False,
    )
```

```python
import math

import jax
import jax.numpy as jnp
from jax import lax
from jax.experimental import pallas as pl
from jax.experimental.pallas import tpu as pltpu
from jax.sharding import PartitionSpec as P

BF = jnp.bfloat16
F32 = jnp.float32
MESH = pl.DeviceIdType.MESH

DH = 128
ROWS = 128
HALF = 64
HEADS = 16
NX, NZ = 4, 8
SLOTS = NX * NZ
FEATURES = 8192
GROUP = 4
TQ = GROUP * ROWS
TK = 8 * ROWS
VROWS = 144
COLS = 1024
OUT = 256
BIG = 2.0**100
SCALE = 1.0 / math.sqrt(DH)
EXP2 = SCALE * math.log2(math.e)
N_SEM = 128
VMEM_LIMIT = 48 << 20
TILES = (
    [(0, dx) for dx in range(NX)],
    [(1, 0), (-1, 0), (2, 0), (-2, 0)],
    [(dz, dx) for dx in (1, 3, 2) for dz in (1, -1)],
    [(dz, dx) for dx in (1, 3, 2) for dz in (2, -2)] + [(3, 0), (-3, 0)],
    [(dz, dx) for dx in (1, 3, 2) for dz in (3, -3)] + [(4, 0)],
    [(4, dx) for dx in (1, 3, 2)],
)
SLOT = {(dz % NZ, dx): i for i, (dz, dx) in enumerate(sum(TILES, []))}
FIRST = [SLOT[t[0][0] % NZ, t[0][1]] for t in TILES]
SIZE = [len(t) for t in TILES]
LATE = 5


def ring(i, *dxs):
    return ("arrive", *[(a, i, dx) for dx in dxs for a in ("ku", "kd")])


SCHEDULE = (
    [("arrive", ("kx", 3), ("kx", 1), ("kx", 2))]
    + [("arrive", ("vz", 1), ("vz", -1)), ring(0, 0)]
    + [(0, 0), ("flush",), ring(0, 1, 3, 2), ("arrive", ("vz", 2), ("vz", -2)), ring(1, 0)]
    + [(1, 0), (0, 1), (1, 1), (2, 0), (2, 1), ("arrive", ("vz", 3), ("vz", -3))]
    + [(0, 2), ring(1, 1, 3), (1, 2), ring(1, 2)]
    + [(2, 2), ring(2, 0), (3, 0), (3, 1), ("arrive", ("vz", 4), ("vz", -4))]
    + [(3, 2), (0, 3), ring(2, 1, 3), (1, 3), ring(2, 2)]
    + [(2, 3), (3, 3), (0, 4), (1, 4), (2, 4), (3, 4), ("flush",)]
)


def slot_of(dz, dx):
    return SLOT[dz % NZ, dx % NX]


def device(y, x, z, c):
    return ((y % 4) // 2, (x % NX) * NZ + z % NZ, (y % 2) * 2 + c)


class Traffic:
    def __init__(self, send, recv):
        self.send, self.recv = send, recv
        self.copies = {}
        self.after = {}
        self.need = {}
        self.came = set()
        self.started = []

    def add(self, name, src, dst, to, after=()):
        i = len(self.copies)
        self.copies[name] = pltpu.make_async_remote_copy(
            src_ref=src,
            dst_ref=dst,
            send_sem=self.send.at[i],
            recv_sem=self.recv.at[i],
            device_id=to,
            device_id_type=MESH,
        )
        self.need[name] = set(after)
        for a in after:
            self.after.setdefault(a, []).append(name)

    def start(self, name):
        self.copies[name].start()
        self.started.append(name)

    def arrive(self, *names):
        for name in names:
            if name in self.came:
                continue
            self.came.add(name)
            self.copies[name].wait_recv()
            for child in self.after.get(name, ()):
                self.need[child].discard(name)
                if not self.need[child]:
                    self.start(child)

    def sent(self):
        for name in self.started:
            self.copies[name].wait_send()
        self.started = []


def kernel(
    order_hbm, gain_hbm, q_hbm, k_hbm, v_hbm, w_hbm,
    kv_out, max_out,
    order, gain_ref, kbuf, vt, vin, vown, qs, w, s_buf, s_late, tops, totals, acc_out, parts, got,
    sqbuf, sqgot, mxbuf, mxgot, mx2, mxgot2, send, recv, local,
):
    pp, cp, tp = lax.axis_index("pp"), lax.axis_index("cp"), lax.axis_index("tp")
    y, x, z, c = pp * 2 + tp // 2, cp // NZ, cp % NZ, tp % 2

    barrier = pltpu.get_barrier_semaphore()
    peers = [device(y, x + d, z, c) for d in (1, 2, 3)]
    peers += [device(y, x, z + d, c) for d in (1, 7)]
    peers += [device(y + 2, x, z + d, c) for d in range(NZ)]
    other = y // 2 * 2 + 1 - y % 2
    mates = [device(y, x, z, 1 - c), device(other, x, z, c), device(other, x, z, 1 - c)]
    for d in peers + mates:
        pl.semaphore_signal(barrier, inc=1, device_id=d, device_id_type=MESH)
    vcopy = pltpu.make_async_copy(v_hbm, vin, local.at[1])
    vcopy.start()
    ocopy = pltpu.make_async_copy(order_hbm, order, local.at[2])
    ocopy.start()
    gcopy = pltpu.make_async_copy(gain_hbm, gain_ref, local.at[3])
    gcopy.start()
    wcopy = pltpu.make_async_copy(w_hbm, w, local.at[0])
    wcopy.start()

    t = Traffic(send, recv)

    def ks(dz, dx, lo=0, n=ROWS):
        return kbuf.at[pl.ds(slot_of(dz, dx) * ROWS + lo, n), pl.ds(0, DH)]

    def vs(dz, dx, lo=0, n=DH):
        return vt.at[slot_of(dz, dx), pl.ds(lo, n), :]

    partner = device(y + 2, x, z, c)
    t.add("k", k_hbm, ks(0, 0), partner)
    t.add("v", vown, vs(0, 0), partner)
    for h in range(HEADS):
        t.add(
            ("q", h),
            q_hbm.at[:, pl.ds(h * DH, DH)],
            qs.at[pl.ds(h * ROWS, ROWS), pl.ds(0, DH)],
            partner,
        )
    for d in (1, -1):
        near = device(y, x, z + d, c)
        for i in range(4):
            n, lo = (DH, 0) if i < 3 else (HALF, 0 if d > 0 else HALF)
            src, dst = vs(-i * d, 0, lo, n), vs(-(i + 1) * d, 0, lo, n)
            t.add(("vz", (i + 1) * d), src, dst, near, [("vz", i * d)] if i else ["v"])
    for d in (1, 3, 2):
        t.add(("kx", d), ks(0, 0), ks(0, -d), device(y, x + d, z, c), ["k"])
    for i in range(4):
        for dx in (0, 1, 3, 2):
            first = ["k"] if dx == 0 else [("kx", 4 - dx)]
            n, lo = (ROWS, 0) if i < 3 else (HALF, HALF)
            t.add(
                ("ku", i, dx), ks(-i, dx, 0, n), ks(-i - 1, dx, 0, n),
                device(y, x, z + 1, c), first if i == 0 else [("ku", i - 1, dx)],
            )
            t.add(
                ("kd", i, dx), ks(i, dx, lo, n), ks(i + 1, dx, lo, n),
                device(y, x, z - 1, c), first if i == 0 else [("kd", i - 1, dx)],
            )
    for dz in (0, 1, -1, 2, -2, 3, -3, 4):
        came = ["v"] if dz == 0 else [("vz", 4), ("vz", -4)] if dz == 4 else [("vz", -dz)]
        for d in (1, 3, 2):
            t.add(("vx", dz, d), vs(dz, 0), vs(dz, -d), device(y, x + d, z, c), came)

    pl.semaphore_wait(barrier, len(peers) + len(mates))

    t.start("k")
    t.start(("q", 0))
    vcopy.wait()
    vown[...] = vin[...].astype(F32).T.astype(BF)
    t.start("v")
    for h in range(1, HEADS):
        t.start(("q", h))
    ocopy.wait()
    gcopy.wait()

    row = lax.broadcasted_iota(jnp.int32, (ROWS, DH), 0)
    lane = lax.broadcasted_iota(jnp.int32, (ROWS, DH), 1)
    mine = (lane >= HALF) == (row >= HALF)
    off = lane % HALF
    q_mask = jnp.where(mine & ((off == 0) | (off > row % HALF)), -BIG, 0.0).astype(BF)
    for h in range(HEADS):
        qs[pl.ds(h * ROWS, ROWS), pl.ds(DH, DH)] = q_mask
    hrow = lax.broadcasted_iota(jnp.int32, (HALF, DH), 0)
    hlane = lax.broadcasted_iota(jnp.int32, (HALF, DH), 1)
    hoff = hlane % HALF
    after_all = (hoff == 0).astype(F32)
    in_block = ((hoff == hrow) & (hoff > 0)).astype(F32)
    half_id = jnp.where(hlane < HALF, order[2 * cp], order[2 * cp + 1])

    def masks(dz):
        for dx in range(NX):
            slot = slot_of(dz, dx)
            src = ((x + dx) % NX) * NZ + (z + dz) % NZ
            for b in range(2):
                block = order[2 * src + b]
                k_mask = jnp.where(half_id < block, after_all, jnp.where(half_id == block, in_block, 0.0))
                kbuf[pl.ds(slot * ROWS + b * HALF, HALF), pl.ds(DH, DH)] = k_mask.astype(BF)
            vt[slot, pl.ds(DH, VROWS - DH), :] = jnp.ones((VROWS - DH, ROWS), BF)

    for dz in range(NZ):
        masks(dz)
    sqbuf[...] = jnp.zeros_like(sqbuf)
    mxbuf[...] = jnp.full_like(mxbuf, -BIG)
    mlane = lax.broadcasted_iota(jnp.int32, (8, DH), 1)
    t.arrive("k", "v")

    def score(g, tile, into):
        first, size = FIRST[tile] * ROWS, SIZE[tile] * ROWS
        s = lax.dot_general(
            kbuf[pl.ds(first, size), :], qs[pl.ds(g * TQ, TQ), :],
            (((1,), (1,)), ((), ())), preferred_element_type=F32,
        )
        into[...] = s
        return jnp.max(s, axis=0, keepdims=True)

    def ready(g, tile):
        t.arrive(*[("q", h) for h in range(g * GROUP, (g + 1) * GROUP)])
        for dz, dx in TILES[tile]:
            if dz == 0:
                t.arrive("k" if dx == 0 else ("kx", 4 - dx))
            elif dz == 4:
                t.arrive(("ku", 3, dx), ("kd", 3, dx))
            else:
                t.arrive(("kd" if dz > 0 else "ku", abs(dz) - 1, dx))

    def ready_v(tile):
        for dz, dx in TILES[tile]:
            t.arrive(*(["v"] if dz == 0 else [("vz", 4), ("vz", -4)] if dz == 4 else [("vz", -dz)]))
            if dx:
                t.arrive(("vx", dz, 4 - dx))

    def weigh(g, first, size, scores, top, ahead=()):
        p = jnp.exp2((scores[...] - top) * EXP2).astype(BF)
        peaks = [score(*a) for a in ahead]
        values = jnp.concatenate([vt[first + i] for i in range(size)], axis=1)
        part = jnp.dot(values, p, preferred_element_type=F32)
        if g in seen:
            totals[g] = totals[g] * jnp.exp2((tops[g] - top) * EXP2) + part
        else:
            totals[g] = part
        tops[g] = top
        seen.add(g)
        return peaks

    def finish(g):
        total = totals[g]
        attn = (total[:DH, :] * (1.0 / total[DH : DH + 1, :])).astype(BF).astype(F32)
        square = jnp.sum(attn * attn, axis=0, keepdims=True)
        pieces = []
        for i in range(GROUP):
            cut = slice(i * ROWS, (i + 1) * ROWS)
            sqbuf[...] += jnp.broadcast_to(square[:, cut], (8, ROWS))
            gain = gain_ref[:, pl.ds((g * GROUP + i) * DH, DH)].astype(F32)
            pieces.append((attn[:, cut].T * gain).astype(BF))
        normed = jnp.concatenate(pieces, axis=1)
        if g < groups - 1:
            product = jnp.dot(normed, w[pl.ds(g * TQ, TQ), :], preferred_element_type=F32)
            acc_out[...] = product if g == 0 else acc_out[...] + product
            return
        for i, to in reversed(list(enumerate(mates))):
            t.add(("sq", i), sqbuf, sqgot.at[i], to)
            t.start(("sq", i))
        for i, dest in ((2, mates[2][2]), (1, mates[1][2]), (0, mates[0][2]), (3, tp)):
            cut = pl.ds(pl.multiple_of(dest * OUT, OUT), OUT)
            product = jnp.dot(normed, w[pl.ds(g * TQ, TQ), cut], preferred_element_type=F32)
            if i == 3:
                acc_out[:, cut] = acc_out[:, cut] + product
                return
            parts[i] = (acc_out[:, cut] + product).astype(BF)
            t.add(("rs", i), parts.at[i], got.at[i], mates[i])
            t.start(("rs", i))

    def largest(g, top):
        for i in range(GROUP):
            best = jnp.max(top[:, i * ROWS : (i + 1) * ROWS], axis=1, keepdims=True) * SCALE
            mxbuf[...] = jnp.where(mlane == g * GROUP + i, best, mxbuf[...])

    def buffer(n, tile):
        return s_buf.at[n % 2, pl.ds(0, SIZE[tile] * ROWS), :]

    groups = HEADS // GROUP
    steps = [i for i in SCHEDULE if isinstance(i[0], int)]
    seen = set()
    n = 0
    peak = None
    for k, item in enumerate(SCHEDULE):
        if item[0] == "arrive":
            t.arrive(*item[1:])
        if not isinstance(item[0], int):
            continue
        g, tile = item
        if peak is None:
            ready(g, tile)
            peak = score(g, tile, buffer(n, tile))
        ready_v(tile)
        ahead = []
        if SCHEDULE[k + 1][0] != "flush":
            ready(*steps[n + 1])
            ahead = [(*steps[n + 1], buffer(n + 1, steps[n + 1][1]))]
        top = jnp.maximum(tops[g], peak) if g in seen else peak
        peaks = weigh(g, FIRST[tile], SIZE[tile], buffer(n, tile), top, ahead)
        peak = peaks[0] if peaks else None
        n += 1
    late_tops = []
    for g in range(groups):
        ready(g, LATE)
        late_tops.append(jnp.maximum(tops[g], score(g, LATE, s_late.at[g])))
        largest(g, late_tops[g])
    for d in (1, 2, 3):
        t.add(("mx", d), mxbuf, mxgot.at[d], device(y, x + d, z, c))
        t.start(("mx", d))
    ready_v(LATE)
    wcopy.wait()
    for g in range(groups):
        weigh(g, FIRST[LATE], SIZE[LATE], s_late.at[g], late_tops[g])
        finish(g)

    t.arrive(*[("mx", d) for d in (1, 2, 3)])
    mx2[...] = jnp.maximum(jnp.maximum(mxbuf[...], mxgot[1]), jnp.maximum(mxgot[2], mxgot[3]))
    for d in range(NZ):
        t.add(("mz", d), mx2, mxgot2.at[d], device(y + 2, x, z + d, c))
        t.start(("mz", d))
    t.sent()
    t.arrive(*[(a, i) for i in range(3) for a in ("sq", "rs")])
    square = sqbuf[...] + sqgot[0] + sqgot[1] + sqgot[2]
    inverse = lax.rsqrt(square * (1.0 / FEATURES) + 1e-05)
    inverse = jnp.broadcast_to(inverse[:1, :], (ROWS, ROWS)).T
    own = acc_out[:, pl.ds(pl.multiple_of(tp * OUT, OUT), OUT)]
    result = own + got[0].astype(F32) + got[1].astype(F32) + got[2].astype(F32)
    kv_out[...] = (result * jnp.concatenate([inverse, inverse], axis=1)).astype(BF)
    t.arrive(*[("mz", d) for d in range(NZ)])
    best = mxgot2[0]
    for d in range(1, NZ):
        best = jnp.maximum(best, mxgot2[d])
    max_out[...] = best[:1, :HEADS]


def on_device(queries, key_vectors, value_vectors, block_order, norm_gain, kv_weight):
    hbm = pl.BlockSpec(memory_space=pltpu.HBM)
    vmem = pl.BlockSpec(memory_space=pltpu.VMEM)
    kv, peak = pl.pallas_call(
        kernel,
        out_shape=(jax.ShapeDtypeStruct((ROWS, OUT), BF), jax.ShapeDtypeStruct((1, HEADS), F32)),
        in_specs=[hbm] * 6,
        out_specs=(vmem, vmem),
        scratch_shapes=[
            pltpu.SMEM((2 * SLOTS,), jnp.int32),
            pltpu.VMEM((1, HEADS * DH), BF),
            pltpu.VMEM((SLOTS * ROWS, 2 * DH), BF),
            pltpu.VMEM((SLOTS, VROWS, ROWS), BF),
            pltpu.VMEM((ROWS, DH), BF),
            pltpu.VMEM((DH, ROWS), BF),
            pltpu.VMEM((HEADS * ROWS, 2 * DH), BF),
            pltpu.VMEM((HEADS * DH, COLS), BF),
            pltpu.VMEM((2, TK, TQ), F32),
            pltpu.VMEM((HEADS // GROUP, SIZE[LATE] * ROWS, TQ), F32),
            pltpu.VMEM((HEADS // GROUP, 1, TQ), F32),
            pltpu.VMEM((HEADS // GROUP, VROWS, TQ), F32),
            pltpu.VMEM((ROWS, COLS), F32),
            pltpu.VMEM((3, ROWS, OUT), BF),
            pltpu.VMEM((3, ROWS, OUT), BF),
            pltpu.VMEM((8, DH), F32),
            pltpu.VMEM((3, 8, DH), F32),
            pltpu.VMEM((8, DH), F32),
            pltpu.VMEM((4, 8, DH), F32),
            pltpu.VMEM((8, DH), F32),
            pltpu.VMEM((NZ, 8, DH), F32),
            pltpu.SemaphoreType.DMA((N_SEM,)),
            pltpu.SemaphoreType.DMA((N_SEM,)),
            pltpu.SemaphoreType.DMA((4,)),
        ],
        compiler_params=pltpu.CompilerParams(
            collective_id=0, has_side_effects=True, vmem_limit_bytes=VMEM_LIMIT
        ),
        name="attention",
    )(
        *[
            pltpu.with_memory_space_constraint(a, pltpu.HBM)
            for a in (block_order, norm_gain, queries[0], key_vectors[0], value_vectors[0], kv_weight[0])
        ]
    )
    return peak, kv[None]


def solution(mesh):
    return jax.shard_map(
        on_device,
        mesh=mesh,
        in_specs=(
            P("pp", "cp", "tp"),
            P("pp", "cp", "tp"),
            P("pp", "cp", "tp"),
            P(),
            P("pp", "tp"),
            P("pp", "tp", None),
        ),
        out_specs=(P("pp", "tp"), P("pp", "cp", "tp")),
        check_vma=False,
    )
```

```python
import math

import jax
import jax.numpy as jnp
from jax import lax
from jax.experimental import pallas as pl
from jax.experimental.pallas import tpu as pltpu
from jax.sharding import PartitionSpec as P

BF = jnp.bfloat16
F32 = jnp.float32
MESH = pl.DeviceIdType.MESH

DH = 128
ROWS = 128
HALF = 64
HEADS = 16
NX, NZ = 4, 8
SLOTS = NX * NZ
FEATURES = 8192
GROUP = 4
TQ = GROUP * ROWS
TK = 8 * ROWS
VROWS = 144
COLS = 1024
OUT = 256
BIG = 2.0**100
SCALE = 1.0 / math.sqrt(DH)
EXP2 = SCALE * math.log2(math.e)
N_SEM = 128
VMEM_LIMIT = 48 << 20
TILES = (
    [(0, dx) for dx in range(NX)],
    [(1, 0), (-1, 0), (2, 0), (-2, 0)],
    [(dz, dx) for dx in (1, 3, 2) for dz in (1, -1)],
    [(dz, dx) for dx in (1, 3, 2) for dz in (2, -2)] + [(3, 0), (-3, 0)],
    [(dz, dx) for dx in (1, 3, 2) for dz in (3, -3)] + [(4, 0)],
    [(4, dx) for dx in (1, 3, 2)],
)
SLOT = {(dz % NZ, dx): i for i, (dz, dx) in enumerate(sum(TILES, []))}
FIRST = [SLOT[t[0][0] % NZ, t[0][1]] for t in TILES]
SIZE = [len(t) for t in TILES]
LATE = 5


def ring(i, *dxs):
    return ("arrive", *[(a, i, dx) for dx in dxs for a in ("ku", "kd")])


SCHEDULE = (
    [("arrive", ("kx", 3), ("kx", 1), ("kx", 2))]
    + [("arrive", ("vz", 1), ("vz", -1)), ring(0, 0)]
    + [(0, 0), ("flush",), ring(0, 1, 3, 2), ("arrive", ("vz", 2), ("vz", -2)), ring(1, 0)]
    + [(1, 0), (0, 1), (1, 1), (2, 0), (2, 1), ("arrive", ("vz", 3), ("vz", -3))]
    + [(0, 2), (1, 2), ring(1, 1, 3), (2, 2), ring(1, 2)]
    + [ring(2, 0), (3, 0), (3, 1), ("arrive", ("vz", 4), ("vz", -4))]
    + [(3, 2), (0, 3), (1, 3), ring(2, 1, 3)]
    + [(2, 3), ring(2, 2), (3, 3), (0, 4), (1, 4), (2, 4), (3, 4), ("flush",)]
)


def slot_of(dz, dx):
    return SLOT[dz % NZ, dx % NX]


def device(y, x, z, c):
    return ((y % 4) // 2, (x % NX) * NZ + z % NZ, (y % 2) * 2 + c)


class Traffic:
    def __init__(self, send, recv):
        self.send, self.recv = send, recv
        self.copies = {}
        self.after = {}
        self.need = {}
        self.came = set()
        self.started = []

    def add(self, name, src, dst, to, after=()):
        i = len(self.copies)
        self.copies[name] = pltpu.make_async_remote_copy(
            src_ref=src,
            dst_ref=dst,
            send_sem=self.send.at[i],
            recv_sem=self.recv.at[i],
            device_id=to,
            device_id_type=MESH,
        )
        self.need[name] = set(after)
        for a in after:
            self.after.setdefault(a, []).append(name)

    def start(self, name):
        self.copies[name].start()
        self.started.append(name)

    def arrive(self, *names):
        for name in names:
            if name in self.came:
                continue
            self.came.add(name)
            self.copies[name].wait_recv()
            for child in self.after.get(name, ()):
                self.need[child].discard(name)
                if not self.need[child]:
                    self.start(child)

    def sent(self):
        for name in self.started:
            self.copies[name].wait_send()
        self.started = []


def kernel(
    order_hbm, gain_hbm, q_hbm, k_hbm, v_hbm, w_hbm,
    kv_out, max_out,
    order, gain_ref, kbuf, vt, vin, vown, qs, w, s_buf, s_late, tops, totals, acc_out, parts, got,
    sqbuf, sqgot, mxbuf, mxgot, mx2, mxgot2, send, recv, local,
):
    pp, cp, tp = lax.axis_index("pp"), lax.axis_index("cp"), lax.axis_index("tp")
    y, x, z, c = pp * 2 + tp // 2, cp // NZ, cp % NZ, tp % 2

    vcopy = pltpu.make_async_copy(v_hbm, vin, local.at[1])
    vcopy.start()
    ocopy = pltpu.make_async_copy(order_hbm, order, local.at[2])
    ocopy.start()
    gcopy = pltpu.make_async_copy(gain_hbm, gain_ref, local.at[3])
    gcopy.start()
    barrier = pltpu.get_barrier_semaphore()
    peers = [device(y, x + d, z, c) for d in (1, 2, 3)]
    peers += [device(y, x, z + d, c) for d in (1, 7)]
    peers += [device(y + 2, x, z + d, c) for d in range(NZ)]
    other = y // 2 * 2 + 1 - y % 2
    mates = [device(y, x, z, 1 - c), device(other, x, z, c), device(other, x, z, 1 - c)]
    for d in peers + mates:
        pl.semaphore_signal(barrier, inc=1, device_id=d, device_id_type=MESH)
    wcopy = pltpu.make_async_copy(w_hbm, w, local.at[0])
    wcopy.start()

    vcopy.wait()
    ocopy.wait()
    gcopy.wait()
    vown[...] = vin[...].astype(F32).T.astype(BF)

    t = Traffic(send, recv)

    def ks(dz, dx, lo=0, n=ROWS):
        return kbuf.at[pl.ds(slot_of(dz, dx) * ROWS + lo, n), pl.ds(0, DH)]

    def vs(dz, dx, lo=0, n=DH):
        return vt.at[slot_of(dz, dx), pl.ds(lo, n), :]

    partner = device(y + 2, x, z, c)
    t.add("k", k_hbm, ks(0, 0), partner)
    t.add("v", vown, vs(0, 0), partner)
    for h in range(HEADS):
        t.add(
            ("q", h),
            q_hbm.at[:, pl.ds(h * DH, DH)],
            qs.at[pl.ds(h * ROWS, ROWS), pl.ds(0, DH)],
            partner,
        )
    for d in (1, -1):
        near = device(y, x, z + d, c)
        for i in range(4):
            n, lo = (DH, 0) if i < 3 else (HALF, 0 if d > 0 else HALF)
            src, dst = vs(-i * d, 0, lo, n), vs(-(i + 1) * d, 0, lo, n)
            t.add(("vz", (i + 1) * d), src, dst, near, [("vz", i * d)] if i else ["v"])
    for d in (1, 3, 2):
        t.add(("kx", d), ks(0, 0), ks(0, -d), device(y, x + d, z, c), ["k"])
    for i in range(4):
        for dx in (0, 1, 3, 2):
            first = ["k"] if dx == 0 else [("kx", 4 - dx)]
            n, lo = (ROWS, 0) if i < 3 else (HALF, HALF)
            t.add(
                ("ku", i, dx), ks(-i, dx, 0, n), ks(-i - 1, dx, 0, n),
                device(y, x, z + 1, c), first if i == 0 else [("ku", i - 1, dx)],
            )
            t.add(
                ("kd", i, dx), ks(i, dx, lo, n), ks(i + 1, dx, lo, n),
                device(y, x, z - 1, c), first if i == 0 else [("kd", i - 1, dx)],
            )
    for dz in (0, 1, -1, 2, -2, 3, -3, 4):
        came = ["v"] if dz == 0 else [("vz", 4), ("vz", -4)] if dz == 4 else [("vz", -dz)]
        for d in (1, 3, 2):
            t.add(("vx", dz, d), vs(dz, 0), vs(dz, -d), device(y, x + d, z, c), came)

    pl.semaphore_wait(barrier, len(peers) + len(mates))

    for name in ["k", "v"] + [("q", h) for h in range(HEADS)]:
        t.start(name)

    row = lax.broadcasted_iota(jnp.int32, (ROWS, DH), 0)
    lane = lax.broadcasted_iota(jnp.int32, (ROWS, DH), 1)
    mine = (lane >= HALF) == (row >= HALF)
    off = lane % HALF
    q_mask = jnp.where(mine & ((off == 0) | (off > row % HALF)), -BIG, 0.0).astype(BF)
    for h in range(HEADS):
        qs[pl.ds(h * ROWS, ROWS), pl.ds(DH, DH)] = q_mask
    hrow = lax.broadcasted_iota(jnp.int32, (HALF, DH), 0)
    hlane = lax.broadcasted_iota(jnp.int32, (HALF, DH), 1)
    hoff = hlane % HALF
    after_all = (hoff == 0).astype(F32)
    in_block = ((hoff == hrow) & (hoff > 0)).astype(F32)
    half_id = jnp.where(hlane < HALF, order[2 * cp], order[2 * cp + 1])

    def masks(dz):
        for dx in range(NX):
            slot = slot_of(dz, dx)
            src = ((x + dx) % NX) * NZ + (z + dz) % NZ
            for b in range(2):
                block = order[2 * src + b]
                k_mask = jnp.where(half_id < block, after_all, jnp.where(half_id == block, in_block, 0.0))
                kbuf[pl.ds(slot * ROWS + b * HALF, HALF), pl.ds(DH, DH)] = k_mask.astype(BF)
            vt[slot, pl.ds(DH, VROWS - DH), :] = jnp.ones((VROWS - DH, ROWS), BF)

    for dz in range(NZ):
        masks(dz)
    sqbuf[...] = jnp.zeros_like(sqbuf)
    mxbuf[...] = jnp.full_like(mxbuf, -BIG)
    mlane = lax.broadcasted_iota(jnp.int32, (8, DH), 1)
    t.arrive("k", "v")

    def score(g, tile, into):
        first, size = FIRST[tile] * ROWS, SIZE[tile] * ROWS
        s = lax.dot_general(
            kbuf[pl.ds(first, size), :], qs[pl.ds(g * TQ, TQ), :],
            (((1,), (1,)), ((), ())), preferred_element_type=F32,
        )
        into[...] = s
        return jnp.max(s, axis=0, keepdims=True)

    def ready(g, tile):
        t.arrive(*[("q", h) for h in range(g * GROUP, (g + 1) * GROUP)])
        for dz, dx in TILES[tile]:
            if dz == 0:
                t.arrive("k" if dx == 0 else ("kx", 4 - dx))
            elif dz == 4:
                t.arrive(("ku", 3, dx), ("kd", 3, dx))
            else:
                t.arrive(("kd" if dz > 0 else "ku", abs(dz) - 1, dx))

    def ready_v(tile):
        for dz, dx in TILES[tile]:
            t.arrive(*(["v"] if dz == 0 else [("vz", 4), ("vz", -4)] if dz == 4 else [("vz", -dz)]))
            if dx:
                t.arrive(("vx", dz, 4 - dx))

    def weigh(g, first, size, scores, top, ahead=()):
        p = jnp.exp2((scores[...] - top) * EXP2).astype(BF)
        peaks = [score(*a) for a in ahead]
        values = jnp.concatenate([vt[first + i] for i in range(size)], axis=1)
        part = jnp.dot(values, p, preferred_element_type=F32)
        if g in seen:
            totals[g] = totals[g] * jnp.exp2((tops[g] - top) * EXP2) + part
        else:
            totals[g] = part
        tops[g] = top
        seen.add(g)
        return peaks

    def finish(g):
        total = totals[g]
        attn = (total[:DH, :] * (1.0 / total[DH : DH + 1, :])).astype(BF).astype(F32)
        square = jnp.sum(attn * attn, axis=0, keepdims=True)
        pieces = []
        for i in range(GROUP):
            cut = slice(i * ROWS, (i + 1) * ROWS)
            sqbuf[...] += jnp.broadcast_to(square[:, cut], (8, ROWS))
            gain = gain_ref[:, pl.ds((g * GROUP + i) * DH, DH)].astype(F32)
            pieces.append((attn[:, cut].T * gain).astype(BF))
        normed = jnp.concatenate(pieces, axis=1)
        if g < groups - 1:
            product = jnp.dot(normed, w[pl.ds(g * TQ, TQ), :], preferred_element_type=F32)
            acc_out[...] = product if g == 0 else acc_out[...] + product
            return
        for i, to in reversed(list(enumerate(mates))):
            t.add(("sq", i), sqbuf, sqgot.at[i], to)
            t.start(("sq", i))
        for i, dest in ((2, mates[2][2]), (1, mates[1][2]), (0, mates[0][2]), (3, tp)):
            cut = pl.ds(pl.multiple_of(dest * OUT, OUT), OUT)
            product = jnp.dot(normed, w[pl.ds(g * TQ, TQ), cut], preferred_element_type=F32)
            if i == 3:
                acc_out[:, cut] = acc_out[:, cut] + product
                return
            parts[i] = (acc_out[:, cut] + product).astype(BF)
            t.add(("rs", i), parts.at[i], got.at[i], mates[i])
            t.start(("rs", i))

    def largest(g, top):
        for i in range(GROUP):
            best = jnp.max(top[:, i * ROWS : (i + 1) * ROWS], axis=1, keepdims=True) * SCALE
            mxbuf[...] = jnp.where(mlane == g * GROUP + i, best, mxbuf[...])

    def buffer(n, tile):
        return s_buf.at[n % 2, pl.ds(0, SIZE[tile] * ROWS), :]

    groups = HEADS // GROUP
    steps = [i for i in SCHEDULE if isinstance(i[0], int)]
    seen = set()
    n = 0
    peak = None
    for k, item in enumerate(SCHEDULE):
        if item[0] == "arrive":
            t.arrive(*item[1:])
        if not isinstance(item[0], int):
            continue
        g, tile = item
        if peak is None:
            ready(g, tile)
            peak = score(g, tile, buffer(n, tile))
        ready_v(tile)
        ahead = []
        if SCHEDULE[k + 1][0] != "flush":
            ready(*steps[n + 1])
            ahead = [(*steps[n + 1], buffer(n + 1, steps[n + 1][1]))]
        top = jnp.maximum(tops[g], peak) if g in seen else peak
        peaks = weigh(g, FIRST[tile], SIZE[tile], buffer(n, tile), top, ahead)
        peak = peaks[0] if peaks else None
        n += 1
    late_tops = []
    for g in range(groups):
        ready(g, LATE)
        late_tops.append(jnp.maximum(tops[g], score(g, LATE, s_late.at[g])))
        largest(g, late_tops[g])
    for d in (1, 2, 3):
        t.add(("mx", d), mxbuf, mxgot.at[d], device(y, x + d, z, c))
        t.start(("mx", d))
    ready_v(LATE)
    wcopy.wait()
    for g in range(groups):
        weigh(g, FIRST[LATE], SIZE[LATE], s_late.at[g], late_tops[g])
        finish(g)

    t.arrive(*[("mx", d) for d in (1, 2, 3)])
    mx2[...] = jnp.maximum(jnp.maximum(mxbuf[...], mxgot[1]), jnp.maximum(mxgot[2], mxgot[3]))
    for d in range(NZ):
        t.add(("mz", d), mx2, mxgot2.at[d], device(y + 2, x, z + d, c))
        t.start(("mz", d))
    t.sent()
    t.arrive(*[(a, i) for i in range(3) for a in ("sq", "rs")])
    square = sqbuf[...] + sqgot[0] + sqgot[1] + sqgot[2]
    inverse = lax.rsqrt(square * (1.0 / FEATURES) + 1e-05)
    inverse = jnp.broadcast_to(inverse[:1, :], (ROWS, ROWS)).T
    own = acc_out[:, pl.ds(pl.multiple_of(tp * OUT, OUT), OUT)]
    result = own + got[0].astype(F32) + got[1].astype(F32) + got[2].astype(F32)
    kv_out[...] = (result * jnp.concatenate([inverse, inverse], axis=1)).astype(BF)
    t.arrive(*[("mz", d) for d in range(NZ)])
    best = mxgot2[0]
    for d in range(1, NZ):
        best = jnp.maximum(best, mxgot2[d])
    max_out[...] = best[:1, :HEADS]


def on_device(queries, key_vectors, value_vectors, block_order, norm_gain, kv_weight):
    hbm = pl.BlockSpec(memory_space=pltpu.HBM)
    vmem = pl.BlockSpec(memory_space=pltpu.VMEM)
    kv, peak = pl.pallas_call(
        kernel,
        out_shape=(jax.ShapeDtypeStruct((ROWS, OUT), BF), jax.ShapeDtypeStruct((1, HEADS), F32)),
        in_specs=[hbm] * 6,
        out_specs=(vmem, vmem),
        scratch_shapes=[
            pltpu.SMEM((2 * SLOTS,), jnp.int32),
            pltpu.VMEM((1, HEADS * DH), BF),
            pltpu.VMEM((SLOTS * ROWS, 2 * DH), BF),
            pltpu.VMEM((SLOTS, VROWS, ROWS), BF),
            pltpu.VMEM((ROWS, DH), BF),
            pltpu.VMEM((DH, ROWS), BF),
            pltpu.VMEM((HEADS * ROWS, 2 * DH), BF),
            pltpu.VMEM((HEADS * DH, COLS), BF),
            pltpu.VMEM((2, TK, TQ), F32),
            pltpu.VMEM((HEADS // GROUP, SIZE[LATE] * ROWS, TQ), F32),
            pltpu.VMEM((HEADS // GROUP, 1, TQ), F32),
            pltpu.VMEM((HEADS // GROUP, VROWS, TQ), F32),
            pltpu.VMEM((ROWS, COLS), F32),
            pltpu.VMEM((3, ROWS, OUT), BF),
            pltpu.VMEM((3, ROWS, OUT), BF),
            pltpu.VMEM((8, DH), F32),
            pltpu.VMEM((3, 8, DH), F32),
            pltpu.VMEM((8, DH), F32),
            pltpu.VMEM((4, 8, DH), F32),
            pltpu.VMEM((8, DH), F32),
            pltpu.VMEM((NZ, 8, DH), F32),
            pltpu.SemaphoreType.DMA((N_SEM,)),
            pltpu.SemaphoreType.DMA((N_SEM,)),
            pltpu.SemaphoreType.DMA((4,)),
        ],
        compiler_params=pltpu.CompilerParams(
            collective_id=0, has_side_effects=True, vmem_limit_bytes=VMEM_LIMIT
        ),
        name="attention",
    )(
        *[
            pltpu.with_memory_space_constraint(a, pltpu.HBM)
            for a in (block_order, norm_gain, queries[0], key_vectors[0], value_vectors[0], kv_weight[0])
        ]
    )
    return peak, kv[None]


def solution(mesh):
    return jax.shard_map(
        on_device,
        mesh=mesh,
        in_specs=(
            P("pp", "cp", "tp"),
            P("pp", "cp", "tp"),
            P("pp", "cp", "tp"),
            P(),
            P("pp", "tp"),
            P("pp", "tp", None),
        ),
        out_specs=(P("pp", "tp"), P("pp", "cp", "tp")),
        check_vma=False,
    )
```
